256 devices in a mesh: gx: 16 (over z, core), gy: 16 (over x, y).
Axes of the slice: x: 4, y: 4, z: 8, core: 2. Of those that a mesh axis runs over, the one named last changes fastest.
Arguments:
- pressure: float32 [4096, 4096], P('gx', 'gy'), may hold values from -6 to 6
- source: float32 [4096, 4096], P('gx', 'gy'), may hold values from -6 to 6
- conductivity: float32 [4096, 4096], P('gx', 'gy'), may hold values from 0.2 to 5
- storage: float32 [4096, 4096], P('gx', 'gy'), may hold values from 0.2 to 1
Outputs:
- pressure_next: float32 [4096, 4096], P('gx', 'gy')
The draws below stay inside these ranges and needn't reach their ends.
All inputs are finite; a program needn't handle non-finite values.
Results may differ from the reference program's by a relative error of at most 0.0001.
Values sent between devices are 32-bit elements; how exact they have to be, the bound alone decides.
No kernel may reach another device: no remote copies, remote signals or barrier semaphores. Data moves between devices by JAX's collectives and lax.ppermute only.
A program may use at most 128 MiB of HBM per device.

```python
import math
import jax
import jax.numpy as jnp

LEVELS_SPLIT = 4
LEVELS_MERGED = 2
COARSE_SWEEPS = 8
NX = 4096
NY = 4096


def block_levels(own_key, shape, cuts, least, top_value):
    gain, own = 1.0, jax.random.fold_in(own_key, 6)
    for position, blocks in cuts:
        draws = jnp.exp(jax.random.uniform(jax.random.fold_in(own, position), (blocks,), jnp.float32, least / len(cuts), top_value / len(cuts)))
        gain = gain * jnp.repeat(draws, shape[position] // blocks).reshape([-1 if axis == position else 1 for axis in range(len(shape))])
    return gain


def centred(own_key, extent, deviation, limit, split=(), kind=jnp.bfloat16):
    values = deviation * jax.random.normal(own_key, extent, jnp.float32)
    if split:
        values = values * block_levels(own_key, extent, split, -0.22, 0.18)
    return jnp.clip(values, -limit, limit).astype(kind)


def setup_inputs(seed: int = 0) -> dict:
    keys = jax.random.split(jax.random.key(seed), 5)
    return {
        "pressure": centred(keys[0], (NX, NY), 1.0, 6.0, ((0, 16), (1, 16)), jnp.float32),
        "source": centred(keys[1], (NX, NY), 1.0, 6.0, ((0, 16), (1, 16)), jnp.float32),
        "conductivity": jnp.clip(jnp.exp(math.log(5.0) - 3.218876 * jax.random.uniform(keys[2], (NX, NY), jnp.float32) ** block_levels(keys[2], (NX, NY), ((0, 16), (1, 16)), -0.2, 0.2)), 0.2, 5.0),
        "storage": jnp.clip(0.2 + 0.8 * jax.random.uniform(keys[3], (NX, NY), jnp.float32) ** block_levels(keys[3], (NX, NY), ((0, 16), (1, 16)), -0.2, 0.2), 0.2, 1.0),
    }


OMEGA = 0.8


def coarsen(grid):
    height, breadth = grid.shape
    return grid.reshape(height // 2, 2, breadth // 2, 2).sum(axis=(1, 3))


def prolong(grid):
    return jnp.repeat(jnp.repeat(grid, 2, axis=0), 2, axis=1)


def face_terms(conduct, stored):
    padded = jnp.pad(conduct, 1)
    west_face = 0.5 * (conduct + padded[:-2, 1:-1])
    east_face = 0.5 * (conduct + padded[2:, 1:-1])
    south_face = 0.5 * (conduct + padded[1:-1, :-2])
    north_face = 0.5 * (conduct + padded[1:-1, 2:])
    diagonal = stored + west_face + east_face + south_face + north_face
    return (diagonal, west_face, east_face, south_face, north_face)


def operate(field, section):
    diagonal, west_face, east_face, south_face, north_face = section
    padded = jnp.pad(field, 1)
    return (diagonal * field - west_face * padded[:-2, 1:-1] - east_face * padded[2:, 1:-1]
            - south_face * padded[1:-1, :-2] - north_face * padded[1:-1, 2:])


def jacobi_sweep(field, right_side, section):
    return field + OMEGA * (right_side - operate(field, section)) / section[0]


def first_sweep(right_side, section):
    return OMEGA * right_side / section[0]


def cycle(sections, depth, right_side, start_field):
    section = sections[depth]
    if depth == len(sections) - 1:
        field = first_sweep(right_side, section)
        for _ in range(COARSE_SWEEPS - 1):
            field = jacobi_sweep(field, right_side, section)
        return field
    if start_field is None:
        field = first_sweep(right_side, section)
    else:
        field = jacobi_sweep(start_field, right_side, section)
    field = jacobi_sweep(field, right_side, section)
    residual = right_side - operate(field, section)
    correction = cycle(sections, depth + 1, coarsen(residual), None)
    field = field + prolong(correction)
    field = jacobi_sweep(field, right_side, section)
    field = jacobi_sweep(field, right_side, section)
    return field


def reference(pressure, source, conductivity, storage):
    conduct, stored = conductivity, storage
    sections = []
    for depth in range(LEVELS_SPLIT + LEVELS_MERGED):
        if depth > 0:
            conduct = 0.5 * coarsen(conduct)
            stored = coarsen(stored)
        sections.append(face_terms(conduct, stored))
    return cycle(sections, 0, source, pressure)
```

```python
import jax
import jax.numpy as jnp
from jax import lax
from jax.experimental import pallas as pl
from jax.experimental.pallas import tpu as pltpu
from jax.sharding import PartitionSpec as P

OMEGA = 0.8
COARSE_SWEEPS = 8
SIZE = 256
HALO = 96
FRAME = 512
PAD = 8
LANES = 128
MIB = 1 << 20


def iota(axis):
    return lax.broadcasted_iota(jnp.int32, (8, LANES), axis)


def roll(x, amount, axis):
    return pltpu.roll(x, amount % x.shape[axis], axis)


def row_shift(tiles):
    row = iota(0)
    down = [roll(x, 1, 0) for x in tiles[:-1]]
    up = [roll(x, -1, 0) for x in tiles[1:]]
    before = [jnp.where(row == 0, down[j], down[j + 1]) for j in range(len(down) - 1)]
    after = [jnp.where(row == 7, up[j + 1], up[j]) for j in range(len(up) - 1)]
    return before, after


def lane_shift(tiles, step):
    lane = iota(1)
    right = [roll(x, step, 1) for x in tiles]
    left = [roll(x, -step, 1) for x in tiles]
    count = len(tiles)
    before = [jnp.where(lane < step, right[t - 1], right[t]) for t in range(count)]
    after = [jnp.where(lane >= LANES - step, left[(t + 1) % count], left[t]) for t in range(count)]
    return before, after


def around(ref, row, depth, step):
    count = ref.shape[0]
    rows = [[ref[t, pl.ds(row + 8 * j - 8, 8), :] for j in range(depth + 2)] for t in range(count)]
    west, east = zip(*[row_shift(tiles) for tiles in rows])
    cells = {}
    for j in range(depth):
        here = [rows[t][j + 1] for t in range(count)]
        south, north = lane_shift(here, step)
        for t in range(count):
            cells[t, j] = (here[t], west[t][j], east[t][j], south[t], north[t])
    return cells


def over_rows(first, last, depth, body):
    trips = (last - first) // (8 * depth)

    def trip(i, carry):
        body(pl.multiple_of(first + i * 8 * depth, 8))
        return carry

    lax.fori_loop(0, trips, trip, 0)


def rows_at(row, j):
    return pl.ds(row + 8 * j, 8)


def face_pass(level, first, last, depth, guess=None):
    def body(row):
        cells = None if guess is None else around(guess, row, depth, level["step"])
        for (t, j), (k, kw, ke, ks, kn) in around(level["k"], row, depth, level["step"]).items():
            at = rows_at(row, j)
            west, east, south, north = (0.5 * (k + other) for other in (kw, ke, ks, kn))
            stored = level["s"][t, at, :]
            diagonal = (((stored + west) + east) + south) + north
            scale = jnp.where(stored > 0.0, OMEGA / diagonal, 0.0)
            level["d"][t, at, :] = diagonal
            side = scale * level["b"][t, at, :]
            level["b"][t, at, :] = side
            weights = [scale * face for face in (west, east, south, north)]
            for name, weight in zip("weon", weights):
                level[name][t, at, :] = weight
            if cells:
                v, *others = cells[t, j]
                side = side + (1.0 - OMEGA) * v
                for weight, other in zip(weights, others):
                    side = side + weight * other
            level["u"][t, at, :] = side

    over_rows(first, last, depth, body)


def weighted(level, t, at, cell):
    _, vw, ve, vs, vn = cell
    total = level["b"][t, at, :] + level["w"][t, at, :] * vw
    total = total + level["e"][t, at, :] * ve
    total = total + level["o"][t, at, :] * vs
    return total + level["n"][t, at, :] * vn


def sweep_pass(level, source, target, first, last, depth):
    def body(row):
        for (t, j), cell in around(source, row, depth, level["step"]).items():
            at = rows_at(row, j)
            target[t, at, :] = (1.0 - OMEGA) * cell[0] + weighted(level, t, at, cell)

    over_rows(first, last, depth, body)


def residual_pass(level, source, target, first, last, depth):
    def body(row):
        for (t, j), cell in around(source, row, depth, level["step"]).items():
            at = rows_at(row, j)
            gap = (1.0 / OMEGA) * weighted(level, t, at, cell) - cell[0]
            target[t, at, :] = level["d"][t, at, :] * gap

    over_rows(first, last, depth, body)


def pair_sum(source, t, row, step):
    x = source[t, pl.ds(row, 8, stride=2), :] + source[t, pl.ds(row + 1, 8, stride=2), :]
    upper = (iota(1) & step) != 0
    return x + jnp.where(upper, roll(x, step, 1), roll(x, -step, 1))


def coarsen_pass(triples, step, first, last):
    height = 2 if (last - first) % 16 == 0 else 1

    def body(row):
        for j in range(height):
            for source, target, factor in triples:
                for t in range(source.shape[0]):
                    x = pair_sum(source, t, 2 * row + 16 * j + PAD, step)
                    target[t, rows_at(row + PAD, j), :] = x if factor == 1.0 else factor * x

    over_rows(first, last, height, body)


def correct_pass(source, base, target, first, last, shift):
    def body(row):
        for t in range(source.shape[0]):
            x = source[t, pl.ds(row, 8), :]
            for half in range(2):
                at = pl.ds(2 * row - shift + half, 8, stride=2)
                target[t, at, :] = base[t, at, :] + x

    over_rows(first, last, 1, body)


def clear_rows(refs, at):
    for ref in refs:
        for row in at:
            for t in range(ref.shape[0]):
                ref[t, pl.ds(row, 8), :] = jnp.zeros((8, LANES), jnp.float32)


def pack_kernel(k, s, b, v, own, low, high, sems):
    copies = []
    for i, a in enumerate((k, s, b, v)):
        for t in range(2):
            copies.append(pltpu.make_async_copy(a.at[:, pl.ds(LANES * t, LANES)], own.at[i, t], sems.at[2 * i + t]))
    for copy in copies:
        copy.start()
    for copy in copies:
        copy.wait()

    def body(row):
        lane = iota(1)
        for j in range(2):
            at = rows_at(row, j)
            x = [own[i, 0, at, :] for i in range(4)]
            low[0, at, :] = jnp.where(lane < 96, x[0], roll(x[1], 96, 1))
            low[1, at, :] = jnp.where(lane < 64, roll(x[1], 96, 1), roll(x[2], 64, 1))
            low[2, at, :] = jnp.where(lane < 32, roll(x[2], 64, 1), roll(x[3], 32, 1))
            y = [own[i, 1, at, :] for i in range(4)]
            high[0, at, :] = jnp.where(lane < 96, roll(y[0], 96, 1), roll(y[1], 64, 1))
            high[1, at, :] = jnp.where(lane < 64, roll(y[1], 64, 1), roll(y[2], 32, 1))
            high[2, at, :] = jnp.where(lane < 32, roll(y[2], 32, 1), y[3])

    over_rows(0, SIZE, 2, body)


def unpack_kernel(own, before, after, middle, top, bottom):
    def widened(row):
        lane = iota(1)
        at = pl.ds(row, 8)
        m = [before[i, at, :] for i in range(3)]
        left = (
            roll(m[0], 32, 1),
            jnp.where(lane < 64, roll(m[0], 64, 1), roll(m[1], 64, 1)),
            jnp.where(lane < 96, roll(m[1], 96, 1), roll(m[2], 96, 1)),
            m[2],
        )
        m = [after[i, at, :] for i in range(3)]
        right = (
            m[0],
            jnp.where(lane < 32, roll(m[0], 32, 1), roll(m[1], 32, 1)),
            jnp.where(lane < 64, roll(m[1], 64, 1), roll(m[2], 64, 1)),
            roll(m[2], 96, 1),
        )
        for i in range(4):
            yield i, 0, jnp.where(lane < 32, 0.0, left[i])
            yield i, 1, own[i, 0, at, :]
            yield i, 2, own[i, 1, at, :]
            yield i, 3, jnp.where(lane < 96, right[i], 0.0)

    def part(target, shift):
        def body(row):
            for i, t, x in widened(row):
                middle[i, t, pl.ds(row, 8), :] = x
                if target is not None:
                    target[i, t, pl.ds(row - shift, 8), :] = x

        return body

    over_rows(0, HALO, 1, part(top, 0))
    over_rows(HALO, SIZE - HALO, 1, part(None, 0))
    over_rows(SIZE - HALO, SIZE, 1, part(bottom, SIZE - HALO))


KEPT = "vbweon"
DOWN = ((32, 480, 4), (16, 240, 4), (8, 120, 2), (0, 64, 4))


def frame_rows(depth):
    return (FRAME >> depth) + 2 * PAD


def down_kernel(middle, above, below, *refs):
    kept, message, refs = refs[0:24], refs[24], refs[25:]
    levels = [dict(zip(KEPT, kept))]
    levels[0].update(zip("ksud", refs[:4]))
    frame = [levels[0][n] for n in "ksbv"]
    for depth in range(1, 4):
        level = dict(zip(KEPT, kept[6 * depth : 6 * depth + 6]))
        level.update(zip("ksud", refs[4 * depth : 4 * depth + 4]))
        levels.append(level)
    last4 = refs[16]

    for depth, (level, (first, last, _)) in enumerate(zip(levels, DOWN)):
        level["step"] = 1 << depth
        clear_rows([level[n] for n in "ksbvuweon"], (PAD + first - 8, PAD + last))

    def fill(row):
        for i in range(4):
            for t in range(4):
                frame[i][t, pl.ds(PAD + 32 + row, 8), :] = above[i, t, pl.ds(row, 8), :]
                frame[i][t, pl.ds(PAD + 384 + row, 8), :] = below[i, t, pl.ds(row, 8), :]

    over_rows(0, HALO, 1, fill)

    def fill_middle(row):
        for i in range(4):
            for t in range(4):
                at = pl.ds(PAD + 128 + row, 8)
                frame[i][t, at, :] = middle[i, t, pl.ds(row, 8), :]

    over_rows(0, SIZE, 1, fill_middle)

    for depth, (level, (first, last, height)) in enumerate(zip(levels, DOWN)):
        v, u = level["v"], level["u"]
        face_pass(level, PAD + first, PAD + last, height, None if depth else v)
        sweep_pass(level, u, v, PAD + first, PAD + last, height)
        residual_pass(level, v, u, PAD + first, PAD + last, height)
        if depth < 3:
            coarse = levels[depth + 1]
            goals = (coarse["k"], coarse["s"], coarse["b"])
            start, stop, _ = DOWN[depth + 1]
        else:
            goals = (last4.at[0], last4.at[1], last4.at[2])
            start, stop = 0, 32
        triples = tuple(zip((level["k"], level["s"], u), goals, (0.5, 1.0, 1.0)))
        coarsen_pass(triples, level["step"], start, stop)

    shape = (LANES, LANES)
    source = lax.broadcasted_iota(jnp.int32, shape, 0)
    goal = lax.broadcasted_iota(jnp.int32, shape, 1)
    for i in range(3):
        total = jnp.zeros((32, LANES), jnp.float32)
        for t in range(4):
            pick = (source + LANES * t == 16 * goal).astype(jnp.float32)
            total = total + jnp.dot(
                last4[i, t, pl.ds(PAD, 32), :],
                pick,
                precision=lax.Precision.HIGHEST,
                preferred_element_type=jnp.float32,
            )
        message[i, :, :] = total


def up_kernel(merged, *refs):
    kept, out, refs = refs[0:24], refs[24], refs[25:]
    four = dict(zip("ksbvudweon", refs[0:10]), step=1)
    five = dict(zip("ksbvudweon", refs[10:20]), step=2)
    levels = [dict(zip(KEPT, kept[6 * depth : 6 * depth + 6])) for depth in range(4)]
    for depth, level in enumerate(levels):
        rows = pl.ds(PAD + (128 >> depth) - 16, (SIZE >> depth) + 32)
        for name in KEPT:
            level[name] = level[name].at[:, rows, :]
        level.update(zip("uc", refs[20 + 2 * depth : 22 + 2 * depth]), step=1 << depth)
    wide = refs[28]

    for i, name in enumerate("ksb"):
        four[name][0, pl.ds(PAD, 64), :] = merged[i]
    clear_rows([four[n] for n in "kvu"], (0, PAD + 64))
    clear_rows([five[n] for n in "kvu"], (0, PAD + 32))
    face_pass(four, PAD, PAD + 64, 4)
    sweep_pass(four, four["u"], four["v"], PAD, PAD + 64, 4)
    residual_pass(four, four["v"], four["u"], PAD, PAD + 64, 4)
    goals = (five["k"], five["s"], five["b"])
    coarsen_pass(tuple(zip((four["k"], four["s"], four["u"]), goals, (0.5, 1.0, 1.0))), 1, 0, 32)
    face_pass(five, PAD, PAD + 32, 4)
    v, u = five["v"], five["u"]
    for _ in range(COARSE_SWEEPS - 1):
        sweep_pass(five, u, v, PAD, PAD + 32, 4)
        v, u = u, v
    correct_pass(u, four["v"], four["v"], PAD, PAD + 32, PAD)
    sweep_pass(four, four["v"], four["u"], PAD, PAD + 64, 4)
    sweep_pass(four, four["u"], four["v"], PAD, PAD + 64, 4)

    shape = (LANES, LANES)
    source = lax.broadcasted_iota(jnp.int32, shape, 0)
    goal = lax.broadcasted_iota(jnp.int32, shape, 1)
    fine = four["v"][0, pl.ds(PAD + 16, 32), :]
    for t in range(4):
        pick = (source == (goal + LANES * t) // 16 + 16).astype(jnp.float32)
        wide[t, pl.ds(0, 32), :] = jnp.dot(
            fine, pick, precision=lax.Precision.HIGHEST, preferred_element_type=jnp.float32
        )

    coarse, first, last, shift = wide, 0, 32, 0
    for depth in (3, 2, 1, 0):
        level = levels[depth]
        size = SIZE >> depth
        u, c = level["u"], level["c"]
        correct_pass(coarse, level["v"], c, first, last, shift)
        sweep_pass(level, c, u, 8, size + 24, 2)
        if depth > 0:
            clear_rows([u], (0, size + 24))
            sweep_pass(level, u, c, 8, size + 24, 2)
            coarse, first, last, shift = c, 8, size + 24, 16

    level = levels[0]

    def body(row):
        for (t, j), cell in around(level["u"], row, 2, 1).items():
            if t in (1, 2):
                at = rows_at(row, j)
                value = (1.0 - OMEGA) * cell[0] + weighted(level, t, at, cell)
                out[pl.ds(row + 8 * j - 16, 8), LANES * (t - 1) : LANES * t] = value

    over_rows(16, SIZE + 16, 2, body)


def shape_of(*shape):
    return jax.ShapeDtypeStruct(shape, jnp.float32)


def vmem(*shape):
    return pltpu.VMEM(shape, jnp.float32)


HERE = pl.BlockSpec(memory_space=pltpu.VMEM)
AWAY = pl.BlockSpec(memory_space=pltpu.HBM)


def cost(flops, count):
    return pl.CostEstimate(flops=flops, bytes_accessed=count, transcendentals=0)


def exchange(up_block, down_block, axis):
    count = lax.axis_size(axis)
    up = [(i, i + 1) for i in range(count - 1)]
    down = [(i + 1, i) for i in range(count - 1)]
    return lax.ppermute(up_block, axis, up), lax.ppermute(down_block, axis, down)


def per_device(pressure, source, conductivity, storage):
    blocks = (conductivity, storage, source, pressure)
    own, low, high = pl.pallas_call(
        pack_kernel,
        out_shape=(shape_of(4, 2, SIZE, LANES), shape_of(3, SIZE, LANES), shape_of(3, SIZE, LANES)),
        in_specs=[AWAY] * 4,
        out_specs=(HERE,) * 3,
        scratch_shapes=[pltpu.SemaphoreType.DMA((8,))],
        cost_estimate=cost(2 * MIB, 2 * MIB),
        compiler_params=pltpu.CompilerParams(vmem_limit_bytes=8 * MIB),
    )(*blocks)
    before, after = exchange(high, low, "gy")

    middle, top, bottom = pl.pallas_call(
        unpack_kernel,
        out_shape=(shape_of(4, 4, SIZE, LANES), shape_of(4, 4, HALO, LANES), shape_of(4, 4, HALO, LANES)),
        in_specs=[HERE] * 3,
        out_specs=(HERE,) * 3,
        cost_estimate=cost(4 * MIB, 4 * MIB),
        compiler_params=pltpu.CompilerParams(vmem_limit_bytes=16 * MIB),
    )(own, before, after)
    above, below = exchange(bottom, top, "gx")

    levels = [(4, frame_rows(depth), LANES) for depth in range(4)]
    kept = [shape for shape in levels for _ in range(6)]
    *kept, message = pl.pallas_call(
        down_kernel,
        out_shape=(
            *[shape_of(*shape) for shape in kept],
            shape_of(3, 32, LANES),
        ),
        in_specs=[HERE] * 3,
        out_specs=(HERE,) * 25,
        scratch_shapes=[
            *[vmem(*shape) for shape in levels for _ in range(4)],
            vmem(3, 4, 32 + 2 * PAD, LANES),
        ],
        cost_estimate=cost(40 * MIB, 12 * MIB),
        compiler_params=pltpu.CompilerParams(vmem_limit_bytes=40 * MIB),
    )(middle, above, below)

    left, right = exchange(message, message, "gy")
    wide = jnp.concatenate(
        [left[:, :, 0:20], message[:, :, 4:28], right[:, :, 12:32], jnp.zeros((3, 32, 64), jnp.float32)], axis=2
    )
    upper, lower = exchange(wide, wide, "gx")
    merged = jnp.concatenate([upper[:, 0:20], wide[:, 4:28], lower[:, 12:32]], axis=1)

    return pl.pallas_call(
        up_kernel,
        out_shape=shape_of(SIZE, SIZE),
        in_specs=[HERE] * 25,
        out_specs=HERE,
        scratch_shapes=[
            *[vmem(1, 64 + 2 * PAD, LANES)] * 10,
            *[vmem(1, 32 + 2 * PAD, LANES)] * 10,
            *[vmem(4, (SIZE >> depth) + 32, LANES) for depth in range(4) for _ in range(2)],
            vmem(4, 32, LANES),
        ],
        cost_estimate=cost(40 * MIB, 12 * MIB),
        compiler_params=pltpu.CompilerParams(vmem_limit_bytes=40 * MIB),
    )(merged, *kept)


def solution(mesh):
    placed = (P("gx", "gy"),) * 4
    return jax.shard_map(per_device, mesh=mesh, in_specs=placed, out_specs=P("gx", "gy"), check_vma=False)
```

```python
import jax
import jax.numpy as jnp
from jax import lax
from jax.experimental import pallas as pl
from jax.experimental.pallas import tpu as pltpu
from jax.sharding import PartitionSpec as P

OMEGA = 0.8
COARSE_SWEEPS = 8
SIZE = 256
HALO = 96
FRAME = 512
PAD = 8
LANES = 128
MIB = 1 << 20


def iota(axis):
    return lax.broadcasted_iota(jnp.int32, (8, LANES), axis)


def roll(x, amount, axis):
    return pltpu.roll(x, amount % x.shape[axis], axis)


def row_shift(tiles):
    row = iota(0)
    down = [roll(x, 1, 0) for x in tiles[:-1]]
    up = [roll(x, -1, 0) for x in tiles[1:]]
    before = [jnp.where(row == 0, down[j], down[j + 1]) for j in range(len(down) - 1)]
    after = [jnp.where(row == 7, up[j + 1], up[j]) for j in range(len(up) - 1)]
    return before, after


def lane_shift(tiles, step):
    lane = iota(1)
    right = [roll(x, step, 1) for x in tiles]
    left = [roll(x, -step, 1) for x in tiles]
    count = len(tiles)
    before = [jnp.where(lane < step, right[t - 1], right[t]) for t in range(count)]
    after = [jnp.where(lane >= LANES - step, left[(t + 1) % count], left[t]) for t in range(count)]
    return before, after


def around(ref, row, depth, step):
    count = ref.shape[0]
    rows = [[ref[t, pl.ds(row + 8 * j - 8, 8), :] for j in range(depth + 2)] for t in range(count)]
    west, east = zip(*[row_shift(tiles) for tiles in rows])
    cells = {}
    for j in range(depth):
        here = [rows[t][j + 1] for t in range(count)]
        south, north = lane_shift(here, step)
        for t in range(count):
            cells[t, j] = (here[t], west[t][j], east[t][j], south[t], north[t])
    return cells


def over_rows(first, last, depth, body):
    trips = (last - first) // (8 * depth)

    def trip(i, carry):
        body(pl.multiple_of(first + i * 8 * depth, 8))
        return carry

    lax.fori_loop(0, trips, trip, 0)


def rows_at(row, j):
    return pl.ds(row + 8 * j, 8)


def face_pass(level, first, last, depth, guess=None):
    def body(row):
        cells = None if guess is None else around(guess, row, depth, level["step"])
        for (t, j), (k, kw, ke, ks, kn) in around(level["k"], row, depth, level["step"]).items():
            at = rows_at(row, j)
            west, east, south, north = (0.5 * (k + other) for other in (kw, ke, ks, kn))
            stored = level["s"][t, at, :]
            diagonal = (((stored + west) + east) + south) + north
            scale = jnp.where(stored > 0.0, OMEGA / diagonal, 0.0)
            level["d"][t, at, :] = diagonal
            side = scale * level["b"][t, at, :]
            level["b"][t, at, :] = side
            weights = [scale * face for face in (west, east, south, north)]
            for name, weight in zip("weon", weights):
                level[name][t, at, :] = weight
            if cells:
                v, *others = cells[t, j]
                side = side + (1.0 - OMEGA) * v
                for weight, other in zip(weights, others):
                    side = side + weight * other
            level["u"][t, at, :] = side

    over_rows(first, last, depth, body)


def weighted(level, t, at, cell):
    _, vw, ve, vs, vn = cell
    total = level["b"][t, at, :] + level["w"][t, at, :] * vw
    total = total + level["e"][t, at, :] * ve
    total = total + level["o"][t, at, :] * vs
    return total + level["n"][t, at, :] * vn


def sweep_pass(level, source, target, first, last, depth):
    def body(row):
        for (t, j), cell in around(source, row, depth, level["step"]).items():
            at = rows_at(row, j)
            target[t, at, :] = (1.0 - OMEGA) * cell[0] + weighted(level, t, at, cell)

    over_rows(first, last, depth, body)


def residual_pass(level, source, target, first, last, depth):
    def body(row):
        for (t, j), cell in around(source, row, depth, level["step"]).items():
            at = rows_at(row, j)
            gap = (1.0 / OMEGA) * weighted(level, t, at, cell) - cell[0]
            target[t, at, :] = level["d"][t, at, :] * gap

    over_rows(first, last, depth, body)


def pair_sum(source, t, row, step):
    x = source[t, pl.ds(row, 8, stride=2), :] + source[t, pl.ds(row + 1, 8, stride=2), :]
    upper = (iota(1) & step) != 0
    return x + jnp.where(upper, roll(x, step, 1), roll(x, -step, 1))


def coarsen_pass(triples, step, first, last):
    height = 2 if (last - first) % 16 == 0 else 1

    def body(row):
        for j in range(height):
            for source, target, factor in triples:
                for t in range(source.shape[0]):
                    x = pair_sum(source, t, 2 * row + 16 * j + PAD, step)
                    target[t, rows_at(row + PAD, j), :] = x if factor == 1.0 else factor * x

    over_rows(first, last, height, body)


def correct_pass(source, base, target, first, last, shift):
    def body(row):
        for t in range(source.shape[0]):
            x = source[t, pl.ds(row, 8), :]
            for half in range(2):
                at = pl.ds(2 * row - shift + half, 8, stride=2)
                target[t, at, :] = base[t, at, :] + x

    over_rows(first, last, 1, body)


def clear_rows(refs, at):
    for ref in refs:
        for row in at:
            for t in range(ref.shape[0]):
                ref[t, pl.ds(row, 8), :] = jnp.zeros((8, LANES), jnp.float32)


def pack_kernel(k, s, b, v, own, low, high, sems):
    copies = []
    for i, a in enumerate((k, s, b, v)):
        for t in range(2):
            copies.append(pltpu.make_async_copy(a.at[:, pl.ds(LANES * t, LANES)], own.at[i, t], sems.at[2 * i + t]))
    for copy in copies:
        copy.start()
    for copy in copies:
        copy.wait()

    def body(row):
        lane = iota(1)
        for j in range(2):
            at = rows_at(row, j)
            x = [own[i, 0, at, :] for i in range(4)]
            low[0, at, :] = jnp.where(lane < 96, x[0], roll(x[1], 96, 1))
            low[1, at, :] = jnp.where(lane < 64, roll(x[1], 96, 1), roll(x[2], 64, 1))
            low[2, at, :] = jnp.where(lane < 32, roll(x[2], 64, 1), roll(x[3], 32, 1))
            y = [own[i, 1, at, :] for i in range(4)]
            high[0, at, :] = jnp.where(lane < 96, roll(y[0], 96, 1), roll(y[1], 64, 1))
            high[1, at, :] = jnp.where(lane < 64, roll(y[1], 64, 1), roll(y[2], 32, 1))
            high[2, at, :] = jnp.where(lane < 32, roll(y[2], 32, 1), y[3])

    over_rows(0, SIZE, 2, body)


def unpack_kernel(edges, own, before, after, middle, top, bottom):
    def widened(row):
        lane = iota(1)
        at = pl.ds(row, 8)
        m = [before[i, at, :] for i in range(3)]
        left = (
            roll(m[0], 32, 1),
            jnp.where(lane < 64, roll(m[0], 64, 1), roll(m[1], 64, 1)),
            jnp.where(lane < 96, roll(m[1], 96, 1), roll(m[2], 96, 1)),
            m[2],
        )
        m = [after[i, at, :] for i in range(3)]
        right = (
            m[0],
            jnp.where(lane < 32, roll(m[0], 32, 1), roll(m[1], 32, 1)),
            jnp.where(lane < 64, roll(m[1], 64, 1), roll(m[2], 64, 1)),
            roll(m[2], 96, 1),
        )
        for i in range(4):
            yield i, 0, jnp.where(lane < edges[0], 0.0, left[i])
            yield i, 1, own[i, 0, at, :]
            yield i, 2, own[i, 1, at, :]
            yield i, 3, jnp.where(lane < edges[1], right[i], 0.0)

    def part(target, shift):
        def body(row):
            for i, t, x in widened(row):
                middle[i, t, pl.ds(row, 8), :] = x
                if target is not None:
                    target[i, t, pl.ds(row - shift, 8), :] = x

        return body

    over_rows(0, HALO, 1, part(top, 0))
    over_rows(HALO, SIZE - HALO, 1, part(None, 0))
    over_rows(SIZE - HALO, SIZE, 1, part(bottom, SIZE - HALO))


KEPT = "vbweon"
DOWN = ((32, 480, 4), (16, 240, 4), (8, 120, 2), (0, 64, 4))


def frame_rows(depth):
    return (FRAME >> depth) + 2 * PAD


def down_kernel(edges, middle, above, below, *refs):
    kept, message, refs = refs[0:24], refs[24], refs[25:]
    levels = [dict(zip(KEPT, kept))]
    levels[0].update(zip("ksud", refs[:4]))
    frame = [levels[0][n] for n in "ksbv"]
    for depth in range(1, 4):
        level = dict(zip(KEPT, kept[6 * depth : 6 * depth + 6]))
        level.update(zip("ksud", refs[4 * depth : 4 * depth + 4]))
        levels.append(level)
    last4 = refs[16]

    for depth, (level, (first, last, _)) in enumerate(zip(levels, DOWN)):
        level["step"] = 1 << depth
        clear_rows([level[n] for n in "ksbvuweon"], (PAD + first - 8, PAD + last))

    def fill(row):
        lane = iota(1)
        for i in range(4):
            for t in range(4):
                at = pl.ds(row, 8)
                frame[i][t, pl.ds(PAD + 32 + row, 8), :] = jnp.where(lane < edges[2], above[i, t, at, :], 0.0)
                frame[i][t, pl.ds(PAD + 384 + row, 8), :] = jnp.where(lane < edges[3], below[i, t, at, :], 0.0)

    over_rows(0, HALO, 1, fill)

    def fill_middle(row):
        for i in range(4):
            for t in range(4):
                at = pl.ds(PAD + 128 + row, 8)
                frame[i][t, at, :] = middle[i, t, pl.ds(row, 8), :]

    over_rows(0, SIZE, 1, fill_middle)

    for depth, (level, (first, last, height)) in enumerate(zip(levels, DOWN)):
        v, u = level["v"], level["u"]
        face_pass(level, PAD + first, PAD + last, height, None if depth else v)
        sweep_pass(level, u, v, PAD + first, PAD + last, height)
        residual_pass(level, v, u, PAD + first, PAD + last, height)
        if depth < 3:
            coarse = levels[depth + 1]
            goals = (coarse["k"], coarse["s"], coarse["b"])
            start, stop, _ = DOWN[depth + 1]
        else:
            goals = (last4.at[0], last4.at[1], last4.at[2])
            start, stop = 0, 32
        triples = tuple(zip((level["k"], level["s"], u), goals, (0.5, 1.0, 1.0)))
        coarsen_pass(triples, level["step"], start, stop)

    shape = (LANES, LANES)
    source = lax.broadcasted_iota(jnp.int32, shape, 0)
    goal = lax.broadcasted_iota(jnp.int32, shape, 1)
    for i in range(3):
        total = jnp.zeros((32, LANES), jnp.float32)
        for t in range(4):
            pick = (source + LANES * t == 16 * goal).astype(jnp.float32)
            total = total + jnp.dot(
                last4[i, t, pl.ds(PAD, 32), :],
                pick,
                precision=lax.Precision.HIGHEST,
                preferred_element_type=jnp.float32,
            )
        message[i, :, :] = total


def up_kernel(merged, *refs):
    kept, out, refs = refs[0:24], refs[24], refs[25:]
    four = dict(zip("ksbvudweon", refs[0:10]), step=1)
    five = dict(zip("ksbvudweon", refs[10:20]), step=2)
    levels = [dict(zip(KEPT, kept[6 * depth : 6 * depth + 6])) for depth in range(4)]
    for depth, level in enumerate(levels):
        rows = pl.ds(PAD + (128 >> depth) - 16, (SIZE >> depth) + 32)
        for name in KEPT:
            level[name] = level[name].at[:, rows, :]
        level.update(zip("uc", refs[20 + 2 * depth : 22 + 2 * depth]), step=1 << depth)
    wide = refs[28]

    for i, name in enumerate("ksb"):
        four[name][0, pl.ds(PAD, 64), :] = merged[i]
    clear_rows([four[n] for n in "kvu"], (0, PAD + 64))
    clear_rows([five[n] for n in "kvu"], (0, PAD + 32))
    face_pass(four, PAD, PAD + 64, 4)
    sweep_pass(four, four["u"], four["v"], PAD, PAD + 64, 4)
    residual_pass(four, four["v"], four["u"], PAD, PAD + 64, 4)
    goals = (five["k"], five["s"], five["b"])
    coarsen_pass(tuple(zip((four["k"], four["s"], four["u"]), goals, (0.5, 1.0, 1.0))), 1, 0, 32)
    face_pass(five, PAD, PAD + 32, 4)
    v, u = five["v"], five["u"]
    for _ in range(COARSE_SWEEPS - 1):
        sweep_pass(five, u, v, PAD, PAD + 32, 4)
        v, u = u, v
    correct_pass(u, four["v"], four["v"], PAD, PAD + 32, PAD)
    sweep_pass(four, four["v"], four["u"], PAD, PAD + 64, 4)
    sweep_pass(four, four["u"], four["v"], PAD, PAD + 64, 4)

    shape = (LANES, LANES)
    source = lax.broadcasted_iota(jnp.int32, shape, 0)
    goal = lax.broadcasted_iota(jnp.int32, shape, 1)
    fine = four["v"][0, pl.ds(PAD + 16, 32), :]
    for t in range(4):
        pick = (source == (goal + LANES * t) // 16 + 16).astype(jnp.float32)
        wide[t, pl.ds(0, 32), :] = jnp.dot(
            fine, pick, precision=lax.Precision.HIGHEST, preferred_element_type=jnp.float32
        )

    coarse, first, last, shift = wide, 0, 32, 0
    for depth in (3, 2, 1, 0):
        level = levels[depth]
        size = SIZE >> depth
        u, c = level["u"], level["c"]
        correct_pass(coarse, level["v"], c, first, last, shift)
        sweep_pass(level, c, u, 8, size + 24, 2)
        if depth > 0:
            clear_rows([u], (0, size + 24))
            sweep_pass(level, u, c, 8, size + 24, 2)
            coarse, first, last, shift = c, 8, size + 24, 16

    level = levels[0]

    def body(row):
        for (t, j), cell in around(level["u"], row, 2, 1).items():
            if t in (1, 2):
                at = rows_at(row, j)
                value = (1.0 - OMEGA) * cell[0] + weighted(level, t, at, cell)
                out[pl.ds(row + 8 * j - 16, 8), LANES * (t - 1) : LANES * t] = value

    over_rows(16, SIZE + 16, 2, body)


def shape_of(*shape):
    return jax.ShapeDtypeStruct(shape, jnp.float32)


def vmem(*shape):
    return pltpu.VMEM(shape, jnp.float32)


HERE = pl.BlockSpec(memory_space=pltpu.VMEM)
SCALARS = pl.BlockSpec(memory_space=pltpu.SMEM)
AWAY = pl.BlockSpec(memory_space=pltpu.HBM)


def cost(flops, count):
    return pl.CostEstimate(flops=flops, bytes_accessed=count, transcendentals=0)


def exchange(up_block, down_block, axis):
    count = lax.axis_size(axis)
    up = [(i, (i + 1) % count) for i in range(count)]
    down = [(j, i) for i, j in up]
    return lax.ppermute(up_block, axis, up), lax.ppermute(down_block, axis, down)


def per_device(pressure, source, conductivity, storage):
    blocks = (conductivity, storage, source, pressure)
    x, y = lax.axis_index("gx"), lax.axis_index("gy")
    inside = (y > 0, y < lax.axis_size("gy") - 1, x > 0, x < lax.axis_size("gx") - 1)
    edges = jnp.stack([jnp.where(here, some, none) for here, some, none in zip(inside, (32, 96, 128, 128), (128, 0, 0, 0))])
    own, low, high = pl.pallas_call(
        pack_kernel,
        out_shape=(shape_of(4, 2, SIZE, LANES), shape_of(3, SIZE, LANES), shape_of(3, SIZE, LANES)),
        in_specs=[AWAY] * 4,
        out_specs=(HERE,) * 3,
        scratch_shapes=[pltpu.SemaphoreType.DMA((8,))],
        cost_estimate=cost(2 * MIB, 2 * MIB),
        compiler_params=pltpu.CompilerParams(vmem_limit_bytes=2 * MIB),
    )(*[pltpu.with_memory_space_constraint(block, pltpu.HBM) for block in blocks])
    before, after = exchange(high, low, "gy")

    middle, top, bottom = pl.pallas_call(
        unpack_kernel,
        out_shape=(shape_of(4, 4, SIZE, LANES), shape_of(4, 4, HALO, LANES), shape_of(4, 4, HALO, LANES)),
        in_specs=[SCALARS] + [HERE] * 3,
        out_specs=(HERE,) * 3,
        cost_estimate=cost(4 * MIB, 4 * MIB),
        compiler_params=pltpu.CompilerParams(vmem_limit_bytes=2 * MIB),
    )(edges, own, before, after)
    above, below = exchange(bottom, top, "gx")

    levels = [(4, frame_rows(depth), LANES) for depth in range(4)]
    kept = [shape for shape in levels for _ in range(6)]
    *kept, message = pl.pallas_call(
        down_kernel,
        out_shape=(
            *[shape_of(*shape) for shape in kept],
            shape_of(3, 32, LANES),
        ),
        in_specs=[SCALARS] + [HERE] * 3,
        out_specs=(HERE,) * 25,
        scratch_shapes=[
            *[vmem(*shape) for shape in levels for _ in range(4)],
            vmem(3, 4, 32 + 2 * PAD, LANES),
        ],
        cost_estimate=cost(40 * MIB, 12 * MIB),
        compiler_params=pltpu.CompilerParams(vmem_limit_bytes=11 * MIB),
    )(edges, middle, above, below)

    left, right = exchange(message, message, "gy")
    left, right = jnp.where(inside[0], left, 0.0), jnp.where(inside[1], right, 0.0)
    wide = jnp.concatenate(
        [left[:, :, 0:20], message[:, :, 4:28], right[:, :, 12:32], jnp.zeros((3, 32, 64), jnp.float32)], axis=2
    )
    upper, lower = exchange(wide, wide, "gx")
    upper, lower = jnp.where(inside[2], upper, 0.0), jnp.where(inside[3], lower, 0.0)
    merged = jnp.concatenate([upper[:, 0:20], wide[:, 4:28], lower[:, 12:32]], axis=1)

    return pl.pallas_call(
        up_kernel,
        out_shape=shape_of(SIZE, SIZE),
        in_specs=[HERE] * 25,
        out_specs=HERE,
        scratch_shapes=[
            *[vmem(1, 64 + 2 * PAD, LANES)] * 10,
            *[vmem(1, 32 + 2 * PAD, LANES)] * 10,
            *[vmem(4, (SIZE >> depth) + 32, LANES) for depth in range(4) for _ in range(2)],
            vmem(4, 32, LANES),
        ],
        cost_estimate=cost(40 * MIB, 12 * MIB),
        compiler_params=pltpu.CompilerParams(vmem_limit_bytes=5 * MIB),
    )(merged, *kept)


def solution(mesh):
    placed = (P("gx", "gy"),) * 4
    return jax.shard_map(per_device, mesh=mesh, in_specs=placed, out_specs=P("gx", "gy"), check_vma=False)
```

```python
import jax
import jax.numpy as jnp
from jax import lax
from jax.experimental import pallas as pl
from jax.experimental.pallas import tpu as pltpu
from jax.sharding import PartitionSpec as P

OMEGA = 0.8
COARSE_SWEEPS = 8
SIZE = 256
HALO = 16
RIM = 24
PAD = 8
LANES = 128
MIB = 1 << 20


def iota(axis):
    return lax.broadcasted_iota(jnp.int32, (8, LANES), axis)


def roll(x, amount, axis):
    return pltpu.roll(x, amount % x.shape[axis], axis)


def row_shift(tiles):
    row = iota(0)
    down = [roll(x, 1, 0) for x in tiles[:-1]]
    up = [roll(x, -1, 0) for x in tiles[1:]]
    before = [jnp.where(row == 0, down[j], down[j + 1]) for j in range(len(down) - 1)]
    after = [jnp.where(row == 7, up[j + 1], up[j]) for j in range(len(up) - 1)]
    return before, after


def lane_shift(tiles, step):
    lane = iota(1)
    right = [roll(x, step, 1) for x in tiles]
    left = [roll(x, -step, 1) for x in tiles]
    count = len(tiles)
    before = [jnp.where(lane < step, right[t - 1], right[t]) for t in range(count)]
    after = [jnp.where(lane >= LANES - step, left[(t + 1) % count], left[t]) for t in range(count)]
    return before, after


def around(ref, row, depth, step):
    count = ref.shape[0]
    rows = [[ref[t, pl.ds(row + 8 * j - 8, 8), :] for j in range(depth + 2)] for t in range(count)]
    west, east = zip(*[row_shift(tiles) for tiles in rows])
    cells = {}
    for j in range(depth):
        here = [rows[t][j + 1] for t in range(count)]
        south, north = lane_shift(here, step)
        for t in range(count):
            cells[t, j] = (here[t], west[t][j], east[t][j], south[t], north[t])
    return cells


def over_rows(first, last, depth, body):
    trips = (last - first) // (8 * depth)

    def trip(i, carry):
        body(pl.multiple_of(first + i * 8 * depth, 8))
        return carry

    lax.fori_loop(0, trips, trip, 0)


def rows_at(row, j):
    return pl.ds(row + 8 * j, 8)


def face_pass(level, first, last, depth, guess=None):
    def body(row):
        cells = None if guess is None else around(guess, row, depth, level["step"])
        for (t, j), (k, kw, ke, ks, kn) in around(level["k"], row, depth, level["step"]).items():
            at = rows_at(row, j)
            west, east, south, north = (0.5 * (k + other) for other in (kw, ke, ks, kn))
            stored = level["s"][t, at, :]
            diagonal = (((stored + west) + east) + south) + north
            scale = jnp.where(stored > 0.0, OMEGA / diagonal, 0.0)
            level["d"][t, at, :] = diagonal
            side = scale * level["b"][t, at, :]
            level["b"][t, at, :] = side
            weights = [scale * face for face in (west, east, south, north)]
            for name, weight in zip("weon", weights):
                level[name][t, at, :] = weight
            if cells:
                v, *others = cells[t, j]
                side = side + (1.0 - OMEGA) * v
                for weight, other in zip(weights, others):
                    side = side + weight * other
            level["u"][t, at, :] = side

    over_rows(first, last, depth, body)


def weighted(level, t, at, cell):
    _, vw, ve, vs, vn = cell
    total = level["b"][t, at, :] + level["w"][t, at, :] * vw
    total = total + level["e"][t, at, :] * ve
    total = total + level["o"][t, at, :] * vs
    return total + level["n"][t, at, :] * vn


def sweep_pass(level, source, target, first, last, depth):
    def body(row):
        for (t, j), cell in around(source, row, depth, level["step"]).items():
            at = rows_at(row, j)
            target[t, at, :] = (1.0 - OMEGA) * cell[0] + weighted(level, t, at, cell)

    over_rows(first, last, depth, body)


def residual_pass(level, source, target, first, last, depth):
    def body(row):
        for (t, j), cell in around(source, row, depth, level["step"]).items():
            at = rows_at(row, j)
            gap = (1.0 / OMEGA) * weighted(level, t, at, cell) - cell[0]
            target[t, at, :] = level["d"][t, at, :] * gap

    over_rows(first, last, depth, body)


def pair_sum(source, t, row, step):
    x = source[t, pl.ds(row, 8, stride=2), :] + source[t, pl.ds(row + 1, 8, stride=2), :]
    upper = (iota(1) & step) != 0
    return x + jnp.where(upper, roll(x, step, 1), roll(x, -step, 1))


def coarsen_pass(triples, step, first, last):
    height = 2 if (last - first) % 16 == 0 else 1

    def body(row):
        for j in range(height):
            for source, target, factor in triples:
                for t in range(source.shape[0]):
                    x = pair_sum(source, t, 2 * row + 16 * j + PAD, step)
                    target[t, rows_at(row + PAD, j), :] = x if factor == 1.0 else factor * x

    over_rows(first, last, height, body)


def correct_pass(source, base, target, first, last, shift):
    def body(row):
        for t in range(source.shape[0]):
            x = source[t, pl.ds(row, 8), :]
            for half in range(2):
                at = pl.ds(2 * row - shift + half, 8, stride=2)
                target[t, at, :] = base[t, at, :] + x

    over_rows(first, last, 1, body)


def clear_rows(refs, at):
    for ref in refs:
        for row in at:
            for t in range(ref.shape[0]):
                ref[t, pl.ds(row, 8), :] = jnp.zeros((8, LANES), jnp.float32)


TILES = (3, 3, 1, 1)
ROWS = (320, 160, 112, 56)
PLACE = (32, 16, RIM, RIM // 2)
STEP = (1, 2, 1, 2)
KEPT = "vbweon"


def array_of(depth):
    return (TILES[depth], ROWS[depth] + 2 * PAD, LANES)


def pack_kernel(k, s, b, v, own, low, high, sems):
    copies = []
    for i, a in enumerate((k, s, b, v)):
        for t in range(2):
            copies.append(pltpu.make_async_copy(a.at[:, pl.ds(LANES * t, LANES)], own.at[i, t], sems.at[2 * i + t]))
    for copy in copies:
        copy.start()
    for copy in copies:
        copy.wait()

    def body(row):
        lane = iota(1)
        for target, t, shift in ((low, 0, 0), (high, 1, HALO)):
            parts = []
            for half in range(2):
                for i in range(4):
                    x = own[i, t, pl.ds(row + 128 * half, 8), :]
                    amount = shift + 64 * half + HALO * i
                    parts.append(roll(x, amount, 1) if amount else x)
            total = parts[7]
            for n in range(6, -1, -1):
                total = jnp.where(lane < HALO * (n + 1), parts[n], total)
            target[pl.ds(row, 8), :] = total

    over_rows(0, 128, 1, body)


def widened(edges, own, before, after, row, half):
    lane = iota(1)
    left = before[pl.ds(row - 128 * half, 8), :]
    right = after[pl.ds(row - 128 * half, 8), :]
    for i in range(4):
        x, y = (roll(own[i, t, pl.ds(row, 8), :], 64, 1) for t in range(2))
        start = 64 * half + HALO * i
        low, high = roll(left, 48 - start, 1), roll(right, 64 - start, 1)
        low = jnp.where(lane < 64 - HALO * edges[0], 0.0, low)
        high = jnp.where(lane < 64 + HALO * edges[1], high, 0.0)
        yield i, 0, jnp.where(lane < 64, low, x)
        yield i, 1, jnp.where(lane < 64, x, y)
        yield i, 2, jnp.where(lane < 64, y, high)


def edge_kernel(edges, own, before, after, top, bottom):
    for j in range(HALO // 8):
        for target, row, half in ((top, 8 * j, 0), (bottom, SIZE - HALO + 8 * j, 1)):
            for i, t, x in widened(edges, own, before, after, row, half):
                target[i, t, pl.ds(8 * j, 8), :] = x


def pick(rule):
    shape = (LANES, LANES)
    rows = lax.broadcasted_iota(jnp.int32, shape, 0)
    columns = lax.broadcasted_iota(jnp.int32, shape, 1)
    return rule(rows, columns).astype(jnp.float32)


def choose(x, chooser):
    return jnp.dot(x, chooser, precision=lax.Precision.HIGHEST, preferred_element_type=jnp.float32)


def smooth_down(level, first, last, height, guess=None):
    face_pass(level, PAD + first, PAD + last, height, guess)
    sweep_pass(level, level["u"], level["v"], PAD + first, PAD + last, height)
    residual_pass(level, level["v"], level["u"], PAD + first, PAD + last, height)


def coarsen_into(level, goals, first, last):
    triples = tuple(zip((level["k"], level["s"], level["u"]), goals, (0.5, 1.0, 1.0)))
    coarsen_pass(triples, level["step"], first, last)


def named_levels(depths, kept, scratch):
    levels = []
    for n, depth in enumerate(depths):
        level = dict(zip(KEPT, kept[6 * n : 6 * n + 6]), step=STEP[depth])
        level.update(zip("ksud", scratch[4 * n : 4 * n + 4]))
        levels.append(level)
    return levels


def fine_kernel(edges, own, before, after, above, below, *refs):
    kept, own2, low2, high2, refs = refs[0:12], refs[12], refs[13], refs[14], refs[15:]
    zero, one = named_levels((0, 1), kept, refs)
    two = refs[8]
    clear_rows([zero[n] for n in "ksbvuweon"], (PAD + 8, PAD + 304))
    clear_rows([one[n] for n in "ksbvuweon"], (PAD, PAD + 152))
    frame = [zero[n] for n in "ksbv"]

    for half in range(2):

        def fill(row):
            for i, t, x in widened(edges, own, before, after, row, half):
                frame[i][t, pl.ds(PAD + 32 + row, 8), :] = x

        over_rows(128 * half, 128 * half + 128, 1, fill)
    lane = iota(1)
    for i in range(4):
        for t in range(3):
            for j in range(HALO // 8):
                at = pl.ds(8 * j, 8)
                up = jnp.where(lane < LANES * edges[2], above[i, t, at, :], 0.0)
                down = jnp.where(lane < LANES * edges[3], below[i, t, at, :], 0.0)
                frame[i][t, pl.ds(PAD + 32 - HALO + 8 * j, 8), :] = up
                frame[i][t, pl.ds(PAD + 32 + SIZE + 8 * j, 8), :] = down

    smooth_down(zero, 16, 304, 4, zero["v"])
    coarsen_into(zero, (one["k"], one["s"], one["b"]), 8, 152)
    smooth_down(one, 8, 152, 6)
    coarsen_into(one, (two.at[0], two.at[1], two.at[2]), 8, 72)

    for i in range(3):
        total = jnp.zeros((64, LANES), jnp.float32)
        for t in range(3):
            chooser = pick(lambda r, c: (r + LANES * t == 64 + 4 * (c - RIM)) & (c >= RIM) & (c < RIM + 64))
            total = total + choose(two[i, t, pl.ds(PAD + 8, 64), :], chooser)
        own2[i, :, :] = total

    def send(row):
        lane = iota(1)
        at = pl.ds(row, 8)
        x = [own2[i, at, :] for i in range(3)]
        for target, start in ((low2, RIM), (high2, 64)):
            y = [roll(x[i], RIM * i - start, 1) for i in range(3)]
            target[at, :] = jnp.where(lane < RIM, y[0], jnp.where(lane < 2 * RIM, y[1], y[2]))

    over_rows(0, 64, 1, send)


def join_kernel(edges, own2, left, right, wide, top, bottom):
    lane = iota(1)
    stop = RIM + 64
    for j in range(8):
        at = pl.ds(8 * j, 8)
        for i in range(3):
            low = roll(left[at, :], -RIM * i, 1)
            high = roll(right[at, :], stop - RIM * i, 1)
            x = jnp.where(lane < RIM * edges[0], low, own2[i, at, :])
            x = jnp.where((lane >= stop) & (lane < stop + RIM * edges[1]), high, x)
            wide[i, at, :] = x
            if 8 * j < RIM:
                top[i, at, :] = x
            if 8 * j >= 64 - RIM:
                bottom[i, pl.ds(8 * j - 64 + RIM, 8), :] = x


def middle_kernel(edges, wide, above, below, *refs):
    kept, message, refs = refs[0:12], refs[12], refs[13:]
    two, three = named_levels((2, 3), kept, refs)
    four = refs[8]
    clear_rows([two[n] for n in "ksbvuweon"], (0, PAD + 112))
    clear_rows([three[n] for n in "ksbvuweon"], (0, PAD + 56))
    lane = iota(1)
    for i, name in enumerate("ksb"):
        for j in range(RIM // 8):
            at = pl.ds(8 * j, 8)
            up = jnp.where(lane < LANES * edges[2], above[i, at, :], 0.0)
            down = jnp.where(lane < LANES * edges[3], below[i, at, :], 0.0)
            two[name][0, pl.ds(PAD + 8 * j, 8), :] = up
            two[name][0, pl.ds(PAD + RIM + 64 + 8 * j, 8), :] = down
        two[name][0, pl.ds(PAD + RIM, 64), :] = wide[i]
    smooth_down(two, 0, 112, 7)
    coarsen_into(two, (three["k"], three["s"], three["b"]), 0, 56)
    smooth_down(three, 0, 56, 7)
    coarsen_into(three, (four.at[0], four.at[1], four.at[2]), 0, 32)
    chooser = pick(lambda r, c: (r == 4 * c) & (c < 28))
    for i in range(3):
        message[i, :, :] = choose(four[i, 0, pl.ds(PAD, 32), :], chooser)


def coarse_join_kernel(edges, message, left, right, wide):
    lane = iota(1)
    for i in range(3):
        for j in range(4):
            at = pl.ds(8 * j, 8)
            low, x, high = roll(left[i, at, :], 2, 1), roll(message[i, at, :], 18, 1), roll(right[i, at, :], 34, 1)
            low = jnp.where((lane >= 2) & (lane < 20 * edges[0]), low, 0.0)
            high = jnp.where(lane < 44 + 18 * edges[1], high, 0.0)
            wide[i, at, :] = jnp.where(lane < 20, low, jnp.where(lane < 44, x, high))


def up_kernel(edges, wide, upper, lower, *refs):
    kept, out, refs = refs[0:24], refs[24], refs[25:]
    four = dict(zip("ksbvudweon", refs[0:10]), step=1)
    five = dict(zip("ksbvudweon", refs[10:20]), step=2)
    levels = [dict(zip(KEPT, kept[6 * depth : 6 * depth + 6])) for depth in range(4)]
    for depth, level in enumerate(levels):
        level.update(zip("uc", refs[20 + 2 * depth : 22 + 2 * depth]), step=STEP[depth])
    from4, coarse_fine = refs[28:30]

    column = lax.broadcasted_iota(jnp.int32, (32, LANES), 1)
    clear_rows([four[n] for n in "ksb"], (PAD, PAD + 56))
    for i, name in enumerate("ksb"):
        four[name][0, pl.ds(PAD + 2, 18), :] = jnp.where(column < LANES * edges[2], upper[i], 0.0)[0:18]
        four[name][0, pl.ds(PAD + 20, 24), :] = wide[i, 2:26, :]
        four[name][0, pl.ds(PAD + 44, 18), :] = jnp.where(column < LANES * edges[3], lower[i], 0.0)[10:28]
    clear_rows([four[n] for n in "kvu"], (0, PAD + 64))
    clear_rows([five[n] for n in "kvu"], (0, PAD + 32))
    smooth_down(four, 0, 64, 4)
    coarsen_into(four, (five["k"], five["s"], five["b"]), 0, 32)
    face_pass(five, PAD, PAD + 32, 4)
    v, u = five["v"], five["u"]
    for _ in range(COARSE_SWEEPS - 1):
        sweep_pass(five, u, v, PAD, PAD + 32, 4)
        v, u = u, v
    correct_pass(u, four["v"], four["v"], PAD, PAD + 32, PAD)
    sweep_pass(four, four["v"], four["u"], PAD, PAD + 64, 4)
    sweep_pass(four, four["u"], four["v"], PAD, PAD + 64, 4)
    from4[0, :, :] = choose(four["v"][0, pl.ds(PAD + 16, 32), :], pick(lambda r, c: r == c // 4 + 18))

    def rise(depth, coarse, first, last, shift, start, stop, height, twice=True):
        level = levels[depth]
        u, c = level["u"], level["c"]
        correct_pass(coarse, level["v"], c, first, last, shift)
        sweep_pass(level, c, u, start, stop, height)
        if twice:
            clear_rows([u], (start - 8, stop))
            sweep_pass(level, u, c, start, stop, height)
        return c

    c = rise(3, from4, 0, 32, -4, 8, 64, 7)
    c = rise(2, c, 8, 64, 8, 24, 104, 5)
    fine = c[0, pl.ds(24, 80), :]
    for t in range(3):
        coarse_fine[t, :, :] = choose(fine, pick(lambda r, c: r == (c + LANES * t) // 4 + 8))
    c = rise(1, coarse_fine, 0, 80, -8, 16, 160, 6)
    rise(0, c, 16, 160, 8, 32, 304, 2, False)

    level = levels[0]

    def body(row):
        lane = iota(1)
        cells = around(level["u"], row, 2, 1)
        for j in range(2):
            values = []
            for t in range(3):
                value = (1.0 - OMEGA) * cells[t, j][0] + weighted(level, t, rows_at(row, j), cells[t, j])
                values.append(roll(value, 64, 1))
            for t in range(2):
                at = pl.ds(row + 8 * j - PAD - 32, 8)
                out[at, LANES * t : LANES * (t + 1)] = jnp.where(lane < 64, values[t], values[t + 1])

    over_rows(PAD + 32, PAD + 32 + SIZE, 2, body)


def shape_of(*shape):
    return jax.ShapeDtypeStruct(shape, jnp.float32)


def vmem(*shape):
    return pltpu.VMEM(shape, jnp.float32)


HERE = pl.BlockSpec(memory_space=pltpu.VMEM)
SCALARS = pl.BlockSpec(memory_space=pltpu.SMEM)
AWAY = pl.BlockSpec(memory_space=pltpu.HBM)


def cost(flops, count):
    return pl.CostEstimate(flops=flops, bytes_accessed=count, transcendentals=0)


def exchange(up_block, down_block, axis):
    count = lax.axis_size(axis)
    up = [(i, (i + 1) % count) for i in range(count)]
    down = [(j, i) for i, j in up]
    return lax.ppermute(up_block, axis, up), lax.ppermute(down_block, axis, down)


def call(kernel, outs, ins, scratch=(), grant=4):
    return pl.pallas_call(
        kernel,
        out_shape=tuple(shape_of(*shape) for shape in outs),
        in_specs=[SCALARS] + [HERE] * (len(ins) - 1),
        out_specs=(HERE,) * len(outs),
        scratch_shapes=scratch,
        cost_estimate=cost(8 * MIB, 4 * MIB),
        compiler_params=pltpu.CompilerParams(vmem_limit_bytes=grant * MIB),
    )(*ins)


def per_device(pressure, source, conductivity, storage):
    blocks = (conductivity, storage, source, pressure)
    x, y = lax.axis_index("gx"), lax.axis_index("gy")
    inside = (y > 0, y < lax.axis_size("gy") - 1, x > 0, x < lax.axis_size("gx") - 1)
    edges = jnp.stack(inside).astype(jnp.int32)
    own, low, high = pl.pallas_call(
        pack_kernel,
        out_shape=(shape_of(4, 2, SIZE, LANES), shape_of(128, LANES), shape_of(128, LANES)),
        in_specs=[AWAY] * 4,
        out_specs=(HERE,) * 3,
        scratch_shapes=[pltpu.SemaphoreType.DMA((8,))],
        cost_estimate=cost(2 * MIB, 2 * MIB),
        compiler_params=pltpu.CompilerParams(vmem_limit_bytes=2 * MIB),
    )(*[pltpu.with_memory_space_constraint(block, pltpu.HBM) for block in blocks])
    before, after = exchange(high, low, "gy")
    top, bottom = call(edge_kernel, [(4, 3, HALO, LANES)] * 2, (edges, own, before, after))
    above, below = exchange(bottom, top, "gx")

    *kept, own2, low2, high2 = call(
        fine_kernel,
        [array_of(0)] * 6 + [array_of(1)] * 6 + [(3, 64, LANES), (64, LANES), (64, LANES)],
        (edges, own, before, after, above, below),
        [vmem(*array_of(0))] * 4 + [vmem(*array_of(1))] * 4 + [vmem(3, 3, 80 + 2 * PAD, LANES)],
        grant=6,
    )
    left, right = exchange(high2, low2, "gy")
    wide2, top2, bottom2 = call(
        join_kernel, [(3, 64, LANES), (3, RIM, LANES), (3, RIM, LANES)], (edges, own2, left, right)
    )
    above2, below2 = exchange(bottom2, top2, "gx")
    *more, message = call(
        middle_kernel,
        [array_of(2)] * 6 + [array_of(3)] * 6 + [(3, 32, LANES)],
        (edges, wide2, above2, below2),
        [vmem(*array_of(2))] * 4 + [vmem(*array_of(3))] * 4 + [vmem(3, 1, 32 + 2 * PAD, LANES)],
    )

    left, right = exchange(message, message, "gy")
    (wide,) = call(coarse_join_kernel, [(3, 32, LANES)], (edges, message, left, right))
    upper, lower = exchange(wide, wide, "gx")
    return pl.pallas_call(
        up_kernel,
        out_shape=shape_of(SIZE, SIZE),
        in_specs=[SCALARS] + [HERE] * 27,
        out_specs=HERE,
        scratch_shapes=[
            *[vmem(1, 64 + 2 * PAD, LANES)] * 10,
            *[vmem(1, 32 + 2 * PAD, LANES)] * 10,
            *[vmem(*array_of(depth)) for depth in range(4) for _ in range(2)],
            vmem(1, 32, LANES),
            vmem(3, 80, LANES),
        ],
        cost_estimate=cost(40 * MIB, 12 * MIB),
        compiler_params=pltpu.CompilerParams(vmem_limit_bytes=5 * MIB),
    )(edges, wide, upper, lower, *kept, *more)


def solution(mesh):
    placed = (P("gx", "gy"),) * 4
    return jax.shard_map(per_device, mesh=mesh, in_specs=placed, out_specs=P("gx", "gy"), check_vma=False)
```

```python
import jax
import jax.numpy as jnp
from jax import lax
from jax.experimental import pallas as pl
from jax.experimental.pallas import tpu as pltpu
from jax.sharding import PartitionSpec as P

OMEGA = 0.8
COARSE_SWEEPS = 8
SIZE = 256
HALO = 16
RIM = 24
PAD = 8
LANES = 128
MIB = 1 << 20


def iota(axis):
    return lax.broadcasted_iota(jnp.int32, (8, LANES), axis)


def roll(x, amount, axis):
    return pltpu.roll(x, amount % x.shape[axis], axis)


def row_shift(tiles):
    row = iota(0)
    down = [roll(x, 1, 0) for x in tiles[:-1]]
    up = [roll(x, -1, 0) for x in tiles[1:]]
    before = [jnp.where(row == 0, down[j], down[j + 1]) for j in range(len(down) - 1)]
    after = [jnp.where(row == 7, up[j + 1], up[j]) for j in range(len(up) - 1)]
    return before, after


def lane_shift(tiles, step):
    lane = iota(1)
    right = [roll(x, step, 1) for x in tiles]
    left = [roll(x, -step, 1) for x in tiles]
    count = len(tiles)
    before = [jnp.where(lane < step, right[t - 1], right[t]) for t in range(count)]
    after = [jnp.where(lane >= LANES - step, left[(t + 1) % count], left[t]) for t in range(count)]
    return before, after


def around(ref, row, depth, step):
    count = ref.shape[0]
    rows = [[ref[t, pl.ds(row + 8 * j - 8, 8), :] for j in range(depth + 2)] for t in range(count)]
    west, east = zip(*[row_shift(tiles) for tiles in rows])
    cells = {}
    for j in range(depth):
        here = [rows[t][j + 1] for t in range(count)]
        south, north = lane_shift(here, step)
        for t in range(count):
            cells[t, j] = (here[t], west[t][j], east[t][j], south[t], north[t])
    return cells


def over_rows(first, last, depth, body):
    trips = (last - first) // (8 * depth)

    def trip(i, carry):
        body(pl.multiple_of(first + i * 8 * depth, 8))
        return carry

    lax.fori_loop(0, trips, trip, 0)


def rows_at(row, j):
    return pl.ds(row + 8 * j, 8)


def face_pass(level, first, last, depth, guess=None):
    def body(row):
        cells = None if guess is None else around(guess, row, depth, level["step"])
        for (t, j), (k, kw, ke, ks, kn) in around(level["k"], row, depth, level["step"]).items():
            at = rows_at(row, j)
            west, east, south, north = (0.5 * (k + other) for other in (kw, ke, ks, kn))
            stored = level["s"][t, at, :]
            diagonal = (((stored + west) + east) + south) + north
            scale = jnp.where(stored > 0.0, OMEGA / diagonal, 0.0)
            level["d"][t, at, :] = diagonal
            side = scale * level["b"][t, at, :]
            level["b"][t, at, :] = side
            weights = [scale * face for face in (west, east, south, north)]
            for name, weight in zip("weon", weights):
                level[name][t, at, :] = weight
            if cells:
                v, *others = cells[t, j]
                side = side + (1.0 - OMEGA) * v
                for weight, other in zip(weights, others):
                    side = side + weight * other
            level["u"][t, at, :] = side

    over_rows(first, last, depth, body)


def weighted(level, t, at, cell):
    _, vw, ve, vs, vn = cell
    total = level["b"][t, at, :] + level["w"][t, at, :] * vw
    total = total + level["e"][t, at, :] * ve
    total = total + level["o"][t, at, :] * vs
    return total + level["n"][t, at, :] * vn


def sweep_pass(level, source, target, first, last, depth):
    def body(row):
        for (t, j), cell in around(source, row, depth, level["step"]).items():
            at = rows_at(row, j)
            target[t, at, :] = (1.0 - OMEGA) * cell[0] + weighted(level, t, at, cell)

    over_rows(first, last, depth, body)


def residual_pass(level, source, target, first, last, depth):
    def body(row):
        for (t, j), cell in around(source, row, depth, level["step"]).items():
            at = rows_at(row, j)
            gap = (1.0 / OMEGA) * weighted(level, t, at, cell) - cell[0]
            target[t, at, :] = level["d"][t, at, :] * gap

    over_rows(first, last, depth, body)


def pair_sum(source, t, row, step):
    x = source[t, pl.ds(row, 8, stride=2), :] + source[t, pl.ds(row + 1, 8, stride=2), :]
    upper = (iota(1) & step) != 0
    return x + jnp.where(upper, roll(x, step, 1), roll(x, -step, 1))


def coarsen_pass(triples, step, first, last):
    height = 2 if (last - first) % 16 == 0 else 1

    def body(row):
        for j in range(height):
            for source, target, factor in triples:
                for t in range(source.shape[0]):
                    x = pair_sum(source, t, 2 * row + 16 * j + PAD, step)
                    target[t, rows_at(row + PAD, j), :] = x if factor == 1.0 else factor * x

    over_rows(first, last, height, body)


def correct_pass(source, base, target, first, last, shift):
    def body(row):
        for t in range(source.shape[0]):
            x = source[t, pl.ds(row, 8), :]
            for half in range(2):
                at = pl.ds(2 * row - shift + half, 8, stride=2)
                target[t, at, :] = base[t, at, :] + x

    over_rows(first, last, 1, body)


def clear_rows(refs, at):
    for ref in refs:
        for row in at:
            for t in range(ref.shape[0]):
                ref[t, pl.ds(row, 8), :] = jnp.zeros((8, LANES), jnp.float32)


TILES = (3, 3, 1, 1)
ROWS = (320, 160, 112, 56)
PLACE = (32, 16, RIM, RIM // 2)
STEP = (1, 2, 1, 2)
KEPT = "vbweon"


def array_of(depth):
    return (TILES[depth], ROWS[depth] + 2 * PAD, LANES)


def pack_kernel(k, s, b, v, own, low, high, sems):
    copies = []
    for i, a in enumerate((k, s, b, v)):
        for t in range(2):
            copies.append(pltpu.make_async_copy(a.at[:, pl.ds(LANES * t, LANES)], own.at[i, t], sems.at[2 * i + t]))
    for copy in copies:
        copy.start()
    for copy in copies:
        copy.wait()

    def body(row):
        lane = iota(1)
        for target, t, shift in ((low, 0, 0), (high, 1, HALO)):
            parts = []
            for half in range(2):
                for i in range(4):
                    x = own[i, t, pl.ds(row + 128 * half, 8), :]
                    amount = shift + 64 * half + HALO * i
                    parts.append(roll(x, amount, 1) if amount else x)
            total = parts[7]
            for n in range(6, -1, -1):
                total = jnp.where(lane < HALO * (n + 1), parts[n], total)
            target[pl.ds(row, 8), :] = total

    over_rows(0, 128, 1, body)


def widened(edges, own, before, after, row, half):
    lane = iota(1)
    left = before[pl.ds(row - 128 * half, 8), :]
    right = after[pl.ds(row - 128 * half, 8), :]
    for i in range(4):
        start = 64 * half + HALO * i
        low, high = roll(left, -HALO - start, 1), roll(right, -start, 1)
        low = jnp.where(lane >= LANES - HALO * edges[0], low, 0.0)
        yield i, 0, own[i, 0, pl.ds(row, 8), :]
        yield i, 1, own[i, 1, pl.ds(row, 8), :]
        yield i, 2, jnp.where(lane < HALO * edges[1], high, low)


def edge_kernel(edges, own, before, after, top, bottom):
    for j in range(HALO // 8):
        for target, row, half in ((top, 8 * j, 0), (bottom, SIZE - HALO + 8 * j, 1)):
            for i, t, x in widened(edges, own, before, after, row, half):
                target[i, t, pl.ds(8 * j, 8), :] = x


def pick(rule):
    shape = (LANES, LANES)
    rows = lax.broadcasted_iota(jnp.int32, shape, 0)
    columns = lax.broadcasted_iota(jnp.int32, shape, 1)
    return rule(rows, columns).astype(jnp.float32).astype(jnp.bfloat16)


def choose(x, chooser):
    total = None
    for _ in range(3):
        term = x.astype(jnp.bfloat16)
        part = jnp.dot(term, chooser, preferred_element_type=jnp.float32)
        total = part if total is None else total + part
        x = x - term.astype(jnp.float32)
    return total


def smooth_down(level, first, last, height, guess=None):
    face_pass(level, PAD + first, PAD + last, height, guess)
    sweep_pass(level, level["u"], level["v"], PAD + first, PAD + last, height)
    residual_pass(level, level["v"], level["u"], PAD + first, PAD + last, height)


def coarsen_into(level, goals, first, last):
    triples = tuple(zip((level["k"], level["s"], level["u"]), goals, (0.5, 1.0, 1.0)))
    coarsen_pass(triples, level["step"], first, last)


def named_levels(depths, kept, scratch):
    levels = []
    for n, depth in enumerate(depths):
        level = dict(zip(KEPT, kept[6 * n : 6 * n + 6]), step=STEP[depth])
        level.update(zip("ksud", scratch[4 * n : 4 * n + 4]))
        levels.append(level)
    return levels


ALL = KEPT + "ksud"


def start_kernel(edges, own, before, after, *refs):
    zero = dict(zip(ALL, refs), step=STEP[0])
    frame = [zero[n] for n in "ksbv"]
    for half in range(2):

        def fill(row):
            for i, t, x in widened(edges, own, before, after, row, half):
                frame[i][t, pl.ds(PAD + 32 + row, 8), :] = x

        over_rows(128 * half, 128 * half + 128, 1, fill)
    face_pass(zero, PAD + 40, PAD + 280, 5, zero["v"])


def fine_kernel(edges, above, below, *refs):
    started, rest, kept1, own2, low2, high2, refs = refs[10:20], refs[0:10], refs[20:26], *refs[26:29], refs[29:]
    zero = dict(zip(ALL, started), step=STEP[0])
    one = dict(zip(ALL, (*kept1, *refs[:4])), step=STEP[1])
    two = refs[4]
    clear_rows([zero[n] for n in "ksbvuweon"], (PAD + 8, PAD + 304))
    clear_rows([one[n] for n in "ksbvuweon"], (PAD, PAD + 152))
    frame = [zero[n] for n in "ksbv"]
    lane = iota(1)
    for i in range(4):
        for t in range(3):
            for j in range(HALO // 8):
                at = pl.ds(8 * j, 8)
                up = jnp.where(lane < LANES * edges[2], above[i, t, at, :], 0.0)
                down = jnp.where(lane < LANES * edges[3], below[i, t, at, :], 0.0)
                frame[i][t, pl.ds(PAD + 32 - HALO + 8 * j, 8), :] = up
                frame[i][t, pl.ds(PAD + 32 + SIZE + 8 * j, 8), :] = down

    face_pass(zero, PAD + 16, PAD + 40, 3, zero["v"])
    face_pass(zero, PAD + 280, PAD + 304, 3, zero["v"])
    sweep_pass(zero, zero["u"], zero["v"], PAD + 16, PAD + 304, 4)
    residual_pass(zero, zero["v"], zero["u"], PAD + 16, PAD + 304, 4)
    coarsen_into(zero, (one["k"], one["s"], one["b"]), 8, 152)
    smooth_down(one, 8, 152, 6)
    coarsen_into(one, (two.at[0], two.at[1], two.at[2]), 8, 72)

    total = None
    for t in range(2):
        inside = lambda c: (c >= RIM) & (c < RIM + 64)
        chooser = pick(lambda r, c: (r + LANES * t == 4 * (c - RIM)) & inside(c))
        rows = jnp.concatenate([two[i, t, pl.ds(PAD + 8, 64), :] for i in range(3)], axis=0)
        part = choose(rows, chooser)
        total = part if total is None else total + part
    for i in range(3):
        own2[i, :, :] = total[64 * i : 64 * i + 64]

    def send(row):
        lane = iota(1)
        at = pl.ds(row, 8)
        x = [own2[i, at, :] for i in range(3)]
        for target, start in ((low2, RIM), (high2, 64)):
            y = [roll(x[i], RIM * i - start, 1) for i in range(3)]
            target[at, :] = jnp.where(lane < RIM, y[0], jnp.where(lane < 2 * RIM, y[1], y[2]))

    over_rows(0, 64, 1, send)


def join_kernel(edges, own2, left, right, wide, top, bottom):
    lane = iota(1)
    stop = RIM + 64
    for j in range(8):
        at = pl.ds(8 * j, 8)
        for i in range(3):
            low = roll(left[at, :], -RIM * i, 1)
            high = roll(right[at, :], stop - RIM * i, 1)
            x = jnp.where(lane < RIM * edges[0], low, own2[i, at, :])
            x = jnp.where((lane >= stop) & (lane < stop + RIM * edges[1]), high, x)
            wide[i, at, :] = x
            if 8 * j < RIM:
                top[i, at, :] = x
            if 8 * j >= 64 - RIM:
                bottom[i, pl.ds(8 * j - 64 + RIM, 8), :] = x


def middle_kernel(edges, wide, above, below, *refs):
    kept, message, refs = refs[0:12], refs[12], refs[13:]
    two, three = named_levels((2, 3), kept, refs)
    four = refs[8]
    clear_rows([two[n] for n in "ksbvuweon"], (0, PAD + 112))
    clear_rows([three[n] for n in "ksbvuweon"], (0, PAD + 56))
    lane = iota(1)
    for i, name in enumerate("ksb"):
        for j in range(RIM // 8):
            at = pl.ds(8 * j, 8)
            up = jnp.where(lane < LANES * edges[2], above[i, at, :], 0.0)
            down = jnp.where(lane < LANES * edges[3], below[i, at, :], 0.0)
            two[name][0, pl.ds(PAD + 8 * j, 8), :] = up
            two[name][0, pl.ds(PAD + RIM + 64 + 8 * j, 8), :] = down
        two[name][0, pl.ds(PAD + RIM, 64), :] = wide[i]
    smooth_down(two, 0, 112, 7)
    coarsen_into(two, (three["k"], three["s"], three["b"]), 0, 56)
    smooth_down(three, 0, 56, 7)
    coarsen_into(three, (four.at[0], four.at[1], four.at[2]), 0, 32)
    chooser = pick(lambda r, c: (r == 4 * c) & (c < 28))
    total = choose(jnp.concatenate([four[i, 0, pl.ds(PAD, 32), :] for i in range(3)], axis=0), chooser)
    for i in range(3):
        message[i, :, :] = total[32 * i : 32 * i + 32]


def coarse_join_kernel(edges, message, left, right, wide):
    lane = iota(1)
    for i in range(3):
        for j in range(4):
            at = pl.ds(8 * j, 8)
            low, x, high = roll(left[i, at, :], 2, 1), roll(message[i, at, :], 18, 1), roll(right[i, at, :], 34, 1)
            low = jnp.where((lane >= 2) & (lane < 20 * edges[0]), low, 0.0)
            high = jnp.where(lane < 44 + 18 * edges[1], high, 0.0)
            wide[i, at, :] = jnp.where(lane < 20, low, jnp.where(lane < 44, x, high))


def up_kernel(edges, wide, upper, lower, *refs):
    kept, out, refs = refs[0:24], refs[24], refs[25:]
    four = dict(zip("ksbvudweon", refs[0:10]), step=1)
    five = dict(zip("ksbvudweon", refs[10:20]), step=2)
    levels = [dict(zip(KEPT, kept[6 * depth : 6 * depth + 6])) for depth in range(4)]
    for depth, level in enumerate(levels):
        level.update(zip("uc", refs[20 + 2 * depth : 22 + 2 * depth]), step=STEP[depth])
    from4, coarse_fine = refs[28:30]

    column = lax.broadcasted_iota(jnp.int32, (32, LANES), 1)
    clear_rows([four[n] for n in "ksb"], (PAD, PAD + 56))
    for i, name in enumerate("ksb"):
        four[name][0, pl.ds(PAD + 2, 18), :] = jnp.where(column < LANES * edges[2], upper[i], 0.0)[0:18]
        four[name][0, pl.ds(PAD + 20, 24), :] = wide[i, 2:26, :]
        four[name][0, pl.ds(PAD + 44, 18), :] = jnp.where(column < LANES * edges[3], lower[i], 0.0)[10:28]
    clear_rows([four[n] for n in "kvu"], (0, PAD + 64))
    clear_rows([five[n] for n in "kvu"], (0, PAD + 32))
    smooth_down(four, 0, 64, 4)
    coarsen_into(four, (five["k"], five["s"], five["b"]), 0, 32)
    face_pass(five, PAD, PAD + 32, 4)
    v, u = five["v"], five["u"]
    for _ in range(COARSE_SWEEPS - 1):
        sweep_pass(five, u, v, PAD, PAD + 32, 4)
        v, u = u, v
    correct_pass(u, four["v"], four["v"], PAD, PAD + 32, PAD)
    sweep_pass(four, four["v"], four["u"], PAD, PAD + 64, 4)
    sweep_pass(four, four["u"], four["v"], PAD, PAD + 64, 4)
    from4[0, :, :] = choose(four["v"][0, pl.ds(PAD + 16, 32), :], pick(lambda r, c: r == c // 4 + 18))

    def rise(depth, coarse, first, last, shift, start, stop, height, twice=True):
        level = levels[depth]
        u, c = level["u"], level["c"]
        correct_pass(coarse, level["v"], c, first, last, shift)
        sweep_pass(level, c, u, start, stop, height)
        if twice:
            clear_rows([u], (start - 8, stop))
            sweep_pass(level, u, c, start, stop, height)
        return c

    c = rise(3, from4, 0, 32, -4, 8, 64, 7)
    c = rise(2, c, 8, 64, 8, 24, 104, 5)
    fine = c[0, pl.ds(24, 80), :]
    for t in range(3):
        turn = lambda c: jnp.where(c < 64, 0, 96) if t == 2 else 0
        coarse_fine[t, :, :] = choose(fine, pick(lambda r, c: r == (c + LANES * t) // 4 + RIM - turn(c)))
    c = rise(1, coarse_fine, 0, 80, -8, 16, 160, 6)
    rise(0, c, 16, 160, 8, 32, 304, 2, False)

    level = levels[0]

    def body(row):
        cells = around(level["u"], row, 2, 1)
        for j in range(2):
            for t in range(2):
                value = (1.0 - OMEGA) * cells[t, j][0] + weighted(level, t, rows_at(row, j), cells[t, j])
                out[pl.ds(row + 8 * j - PAD - 32, 8), LANES * t : LANES * (t + 1)] = value

    over_rows(PAD + 32, PAD + 32 + SIZE, 2, body)


def shape_of(*shape):
    return jax.ShapeDtypeStruct(shape, jnp.float32)


def vmem(*shape):
    return pltpu.VMEM(shape, jnp.float32)


HERE = pl.BlockSpec(memory_space=pltpu.VMEM)
SCALARS = pl.BlockSpec(memory_space=pltpu.SMEM)
AWAY = pl.BlockSpec(memory_space=pltpu.HBM)


def cost(flops, count):
    return pl.CostEstimate(flops=flops, bytes_accessed=count, transcendentals=0)


def exchange(up_block, down_block, axis):
    count = lax.axis_size(axis)
    up = [(i, (i + 1) % count) for i in range(count)]
    down = [(j, i) for i, j in up]
    return lax.ppermute(up_block, axis, up), lax.ppermute(down_block, axis, down)


def call(kernel, outs, ins, scratch=(), grant=4, aliases={}):
    return pl.pallas_call(
        kernel,
        out_shape=tuple(shape_of(*shape) for shape in outs),
        in_specs=[SCALARS] + [HERE] * (len(ins) - 1),
        out_specs=(HERE,) * len(outs),
        scratch_shapes=scratch,
        input_output_aliases=aliases,
        cost_estimate=cost(8 * MIB, 4 * MIB),
        compiler_params=pltpu.CompilerParams(vmem_limit_bytes=grant * MIB),
    )(*ins)


def per_device(pressure, source, conductivity, storage):
    blocks = (conductivity, storage, source, pressure)
    x, y = lax.axis_index("gx"), lax.axis_index("gy")
    inside = (y > 0, y < lax.axis_size("gy") - 1, x > 0, x < lax.axis_size("gx") - 1)
    edges = jnp.stack(inside).astype(jnp.int32)
    own, low, high = pl.pallas_call(
        pack_kernel,
        out_shape=(shape_of(4, 2, SIZE, LANES), shape_of(128, LANES), shape_of(128, LANES)),
        in_specs=[AWAY] * 4,
        out_specs=(HERE,) * 3,
        scratch_shapes=[pltpu.SemaphoreType.DMA((8,))],
        cost_estimate=cost(2 * MIB, 2 * MIB),
        compiler_params=pltpu.CompilerParams(vmem_limit_bytes=2 * MIB),
    )(*[pltpu.with_memory_space_constraint(block, pltpu.HBM) for block in blocks])
    before, after = exchange(high, low, "gy")
    top, bottom = call(edge_kernel, [(4, 3, HALO, LANES)] * 2, (edges, own, before, after))
    above, below = exchange(bottom, top, "gx")

    started = call(start_kernel, [array_of(0)] * 10, (edges, own, before, after))
    *kept, own2, low2, high2 = call(
        fine_kernel,
        [array_of(0)] * 10 + [array_of(1)] * 6 + [(3, 64, LANES), (64, LANES), (64, LANES)],
        (edges, above, below, *started),
        [vmem(*array_of(1))] * 4 + [vmem(3, 3, 80 + 2 * PAD, LANES)],
        aliases={3 + n: n for n in range(10)},
    )
    kept = kept[:6] + kept[10:]
    left, right = exchange(high2, low2, "gy")
    wide2, top2, bottom2 = call(
        join_kernel, [(3, 64, LANES), (3, RIM, LANES), (3, RIM, LANES)], (edges, own2, left, right)
    )
    above2, below2 = exchange(bottom2, top2, "gx")
    *more, message = call(
        middle_kernel,
        [array_of(2)] * 6 + [array_of(3)] * 6 + [(3, 32, LANES)],
        (edges, wide2, above2, below2),
        [vmem(*array_of(2))] * 4 + [vmem(*array_of(3))] * 4 + [vmem(3, 1, 32 + 2 * PAD, LANES)],
    )

    left, right = exchange(message, message, "gy")
    (wide,) = call(coarse_join_kernel, [(3, 32, LANES)], (edges, message, left, right))
    upper, lower = exchange(wide, wide, "gx")
    return pl.pallas_call(
        up_kernel,
        out_shape=shape_of(SIZE, SIZE),
        in_specs=[SCALARS] + [HERE] * 27,
        out_specs=HERE,
        scratch_shapes=[
            *[vmem(1, 64 + 2 * PAD, LANES)] * 10,
            *[vmem(1, 32 + 2 * PAD, LANES)] * 10,
            *[vmem(*array_of(depth)) for depth in range(4) for _ in range(2)],
            vmem(1, 32, LANES),
            vmem(3, 80, LANES),
        ],
        cost_estimate=cost(40 * MIB, 12 * MIB),
        compiler_params=pltpu.CompilerParams(vmem_limit_bytes=5 * MIB),
    )(edges, wide, upper, lower, *kept, *more)


def solution(mesh):
    placed = (P("gx", "gy"),) * 4
    return jax.shard_map(per_device, mesh=mesh, in_specs=placed, out_specs=P("gx", "gy"), check_vma=False)
```

```python
import jax
import jax.numpy as jnp
from jax import lax
from jax.experimental import pallas as pl
from jax.experimental.pallas import tpu as pltpu
from jax.sharding import PartitionSpec as P

OMEGA = 0.8
COARSE_SWEEPS = 8
SIZE = 256
HALO = 16
RIM = 24
PAD = 8
LANES = 128
MIB = 1 << 20


def iota(axis):
    return lax.broadcasted_iota(jnp.int32, (8, LANES), axis)


def roll(x, amount, axis):
    return pltpu.roll(x, amount % x.shape[axis], axis)


def row_shift(tiles):
    row = iota(0)
    down = [roll(x, 1, 0) for x in tiles[:-1]]
    up = [roll(x, -1, 0) for x in tiles[1:]]
    before = [jnp.where(row == 0, down[j], down[j + 1]) for j in range(len(down) - 1)]
    after = [jnp.where(row == 7, up[j + 1], up[j]) for j in range(len(up) - 1)]
    return before, after


def lane_shift(tiles, step):
    lane = iota(1)
    right = [roll(x, step, 1) for x in tiles]
    left = [roll(x, -step, 1) for x in tiles]
    count = len(tiles)
    before = [jnp.where(lane < step, right[t - 1], right[t]) for t in range(count)]
    after = [jnp.where(lane >= LANES - step, left[(t + 1) % count], left[t]) for t in range(count)]
    return before, after


def around(ref, row, depth, step):
    count = ref.shape[0]
    rows = [[ref[t, pl.ds(row + 8 * j - 8, 8), :] for j in range(depth + 2)] for t in range(count)]
    west, east = zip(*[row_shift(tiles) for tiles in rows])
    cells = {}
    for j in range(depth):
        here = [rows[t][j + 1] for t in range(count)]
        south, north = lane_shift(here, step)
        for t in range(count):
            cells[t, j] = (here[t], west[t][j], east[t][j], south[t], north[t])
    return cells


def over_rows(first, last, depth, body):
    trips = (last - first) // (8 * depth)

    def trip(i, carry):
        body(pl.multiple_of(first + i * 8 * depth, 8))
        return carry

    lax.fori_loop(0, trips, trip, 0)


def rows_at(row, j):
    return pl.ds(row + 8 * j, 8)


def face_pass(level, first, last, depth, guess=None):
    def body(row):
        cells = None if guess is None else around(guess, row, depth, level["step"])
        for (t, j), (k, kw, ke, ks, kn) in around(level["k"], row, depth, level["step"]).items():
            at = rows_at(row, j)
            west, east, south, north = (0.5 * (k + other) for other in (kw, ke, ks, kn))
            stored = level["s"][t, at, :]
            diagonal = (((stored + west) + east) + south) + north
            scale = jnp.where(stored > 0.0, OMEGA / diagonal, 0.0)
            level["d"][t, at, :] = diagonal
            side = scale * level["b"][t, at, :]
            level["b"][t, at, :] = side
            weights = [scale * face for face in (west, east, south, north)]
            for name, weight in zip("weon", weights):
                level[name][t, at, :] = weight
            if cells:
                v, *others = cells[t, j]
                side = side + (1.0 - OMEGA) * v
                for weight, other in zip(weights, others):
                    side = side + weight * other
            level["u"][t, at, :] = side

    over_rows(first, last, depth, body)


def weighted(level, t, at, cell):
    _, vw, ve, vs, vn = cell
    total = level["b"][t, at, :] + level["w"][t, at, :] * vw
    total = total + level["e"][t, at, :] * ve
    total = total + level["o"][t, at, :] * vs
    return total + level["n"][t, at, :] * vn


def sweep_pass(level, source, target, first, last, depth):
    def body(row):
        for (t, j), cell in around(source, row, depth, level["step"]).items():
            at = rows_at(row, j)
            target[t, at, :] = (1.0 - OMEGA) * cell[0] + weighted(level, t, at, cell)

    over_rows(first, last, depth, body)


def residual_pass(level, source, target, first, last, depth):
    def body(row):
        for (t, j), cell in around(source, row, depth, level["step"]).items():
            at = rows_at(row, j)
            gap = (1.0 / OMEGA) * weighted(level, t, at, cell) - cell[0]
            target[t, at, :] = level["d"][t, at, :] * gap

    over_rows(first, last, depth, body)


def pair_sum(source, t, row, step):
    x = source[t, pl.ds(row, 8, stride=2), :] + source[t, pl.ds(row + 1, 8, stride=2), :]
    upper = (iota(1) & step) != 0
    return x + jnp.where(upper, roll(x, step, 1), roll(x, -step, 1))


def coarsen_pass(triples, step, first, last):
    trips = (last - first) // 8
    height = max(n for n in (1, 2, 4, 6, 8) if trips % n == 0)

    def body(row):
        for j in range(height):
            for source, target, factor in triples:
                for t in range(source.shape[0]):
                    x = pair_sum(source, t, 2 * row + 16 * j + PAD, step)
                    target[t, rows_at(row + PAD, j), :] = x if factor == 1.0 else factor * x

    over_rows(first, last, height, body)


def correct_pass(source, base, target, first, last, shift):
    trips = (last - first) // 8
    height = max(n for n in range(1, 8) if trips % n == 0)

    def body(row):
        for j in range(height):
            for t in range(source.shape[0]):
                x = source[t, rows_at(row, j), :]
                for half in range(2):
                    at = pl.ds(2 * row + 16 * j - shift + half, 8, stride=2)
                    target[t, at, :] = base[t, at, :] + x

    over_rows(first, last, height, body)


def clear_rows(refs, at):
    for ref in refs:
        for row in at:
            for t in range(ref.shape[0]):
                ref[t, pl.ds(row, 8), :] = jnp.zeros((8, LANES), jnp.float32)


TILES = (3, 3, 1, 1)
ROWS = (320, 160, 112, 56)
PLACE = (32, 16, RIM, RIM // 2)
STEP = (1, 2, 1, 2)
KEPT = "vbweon"


def array_of(depth):
    return (TILES[depth], ROWS[depth] + 2 * PAD, LANES)


def pack_kernel(k, s, b, v, own, low, high, sems):
    copies = []
    for i, a in enumerate((k, s, b, v)):
        for t in range(2):
            copies.append(pltpu.make_async_copy(a.at[:, pl.ds(LANES * t, LANES)], own.at[i, t], sems.at[2 * i + t]))
    for copy in copies:
        copy.start()
    for copy in copies:
        copy.wait()

    def body(row):
        lane = iota(1)
        for target, t, shift in ((low, 0, 0), (high, 1, HALO)):
            parts = []
            for half in range(2):
                for i in range(4):
                    x = own[i, t, pl.ds(row + 128 * half, 8), :]
                    amount = shift + 64 * half + HALO * i
                    parts.append(roll(x, amount, 1) if amount else x)
            total = parts[7]
            for n in range(6, -1, -1):
                total = jnp.where(lane < HALO * (n + 1), parts[n], total)
            target[pl.ds(row, 8), :] = total

    over_rows(0, 128, 1, body)


def widened(edges, own, before, after, row, half):
    lane = iota(1)
    left = before[pl.ds(row - 128 * half, 8), :]
    right = after[pl.ds(row - 128 * half, 8), :]
    for i in range(4):
        start = 64 * half + HALO * i
        low, high = roll(left, -HALO - start, 1), roll(right, -start, 1)
        low = jnp.where(lane >= LANES - HALO * edges[0], low, 0.0)
        yield i, 0, own[i, 0, pl.ds(row, 8), :]
        yield i, 1, own[i, 1, pl.ds(row, 8), :]
        yield i, 2, jnp.where(lane < HALO * edges[1], high, low)


def edge_kernel(edges, own, before, after, _, top, bottom):
    for j in range(HALO // 8):
        for target, row, half in ((top, 8 * j, 0), (bottom, SIZE - HALO + 8 * j, 1)):
            for i, t, x in widened(edges, own, before, after, row, half):
                target[i, t, pl.ds(8 * j, 8), :] = x


def pick(rule):
    shape = (LANES, LANES)
    rows = lax.broadcasted_iota(jnp.int32, shape, 0)
    columns = lax.broadcasted_iota(jnp.int32, shape, 1)
    return rule(rows, columns).astype(jnp.float32).astype(jnp.bfloat16)


def choose(x, chooser):
    total = None
    for _ in range(3):
        term = x.astype(jnp.bfloat16)
        part = jnp.dot(term, chooser, preferred_element_type=jnp.float32)
        total = part if total is None else total + part
        x = x - term.astype(jnp.float32)
    return total


def smooth_down(level, first, last, height, guess=None):
    face_pass(level, PAD + first, PAD + last, height, guess)
    sweep_pass(level, level["u"], level["v"], PAD + first, PAD + last, height)
    residual_pass(level, level["v"], level["u"], PAD + first, PAD + last, height)


def coarsen_into(level, goals, first, last):
    triples = tuple(zip((level["k"], level["s"], level["u"]), goals, (0.5, 1.0, 1.0)))
    coarsen_pass(triples, level["step"], first, last)


def named_levels(depths, kept, scratch):
    levels = []
    for n, depth in enumerate(depths):
        level = dict(zip(KEPT, kept[6 * n : 6 * n + 6]), step=STEP[depth])
        level.update(zip("ksud", scratch[4 * n : 4 * n + 4]))
        levels.append(level)
    return levels


def shrink_kernel(edges, own, k1, s1, k2, s2):
    def halve(source, target, step, from_row, to_row, count, factor):
        def body(row):
            for j in range(4):
                for t in range(2):
                    x = pair_sum(source, t, 2 * row + 16 * j + from_row, step)
                    target[t, rows_at(row + to_row, j), :] = factor * x

        over_rows(0, count, 4, body)

    for i, first, second, factor in ((0, k1, k2, 0.5), (1, s1, s2, 1.0)):
        halve(own.at[i], first, 1, 0, PAD + 16, 128, factor)
        halve(first, second, 2, PAD + 16, 0, 64, factor)


ALL = KEPT + "ksud"


def start_kernel(edges, own, before, after, *refs):
    zero = dict(zip(ALL, refs), step=STEP[0])
    frame = [zero[n] for n in "ksbv"]
    for half in range(2):

        def fill(row):
            for j in range(4):
                for i, t, x in widened(edges, own, before, after, row + 8 * j, half):
                    frame[i][t, rows_at(PAD + 32 + row, j), :] = x

        over_rows(128 * half, 128 * half + 128, 4, fill)
    face_pass(zero, PAD + 40, PAD + 280, 5, zero["v"])


def fine_kernel(edges, above, below, *refs):
    k2, s2, refs = refs[12], refs[13], refs[14:]
    zero = dict(zip(ALL, refs[0:10]), step=STEP[0])
    own2, low2, high2, u1, d1, b2 = refs[18:24]
    one = dict(zip(ALL, (*refs[10:18], u1, d1)), step=STEP[1])
    clear_rows([zero[n] for n in "ksbvuweon"], (PAD + 8, PAD + 304))
    clear_rows([one[n] for n in "ksbvuweon"], (PAD, PAD + 152))
    frame = [zero[n] for n in "ksbv"]
    lane = iota(1)
    for i in range(4):
        for t in range(3):
            for j in range(HALO // 8):
                at = pl.ds(8 * j, 8)
                up = jnp.where(lane < LANES * edges[2], above[i, t, at, :], 0.0)
                down = jnp.where(lane < LANES * edges[3], below[i, t, at, :], 0.0)
                frame[i][t, pl.ds(PAD + 32 - HALO + 8 * j, 8), :] = up
                frame[i][t, pl.ds(PAD + 32 + SIZE + 8 * j, 8), :] = down

    face_pass(zero, PAD + 16, PAD + 40, 3, zero["v"])
    face_pass(zero, PAD + 280, PAD + 304, 3, zero["v"])
    sweep_pass(zero, zero["u"], zero["v"], PAD + 16, PAD + 304, 12)
    residual_pass(zero, zero["v"], zero["u"], PAD + 16, PAD + 304, 12)
    pairs = [(zero[n], one[n], factor) for n, factor in (("k", 0.5), ("s", 1.0))]
    third = [(source.at[pl.ds(2, 1)], target.at[pl.ds(2, 1)], factor) for source, target, factor in pairs]
    coarsen_pass([(zero["u"], one["b"], 1.0), *third], 1, 8, 152)
    first = [(source.at[pl.ds(0, 2)], target.at[pl.ds(0, 2)], factor) for source, target, factor in pairs]
    coarsen_pass(first, 1, 8, 16)
    coarsen_pass(first, 1, 144, 152)
    smooth_down(one, 8, 152, 6)
    coarsen_pass([(one["u"].at[pl.ds(0, 2)], b2, 1.0)], 2, 8, 72)

    total = None
    for t in range(2):
        inside = lambda c: (c >= RIM) & (c < RIM + 64)
        chooser = pick(lambda r, c: (r + LANES * t == 4 * (c - RIM)) & inside(c))
        rows = jnp.concatenate([k2[t], s2[t], b2[t, pl.ds(PAD + 8, 64), :]], axis=0)
        part = choose(rows, chooser)
        total = part if total is None else total + part
    for i in range(3):
        own2[i, :, :] = total[64 * i : 64 * i + 64]

    def send(row):
        lane = iota(1)
        at = pl.ds(row, 8)
        x = [own2[i, at, :] for i in range(3)]
        for target, start in ((low2, RIM), (high2, 64)):
            y = [roll(x[i], RIM * i - start, 1) for i in range(3)]
            target[at, :] = jnp.where(lane < RIM, y[0], jnp.where(lane < 2 * RIM, y[1], y[2]))

    over_rows(0, 64, 1, send)


def join_kernel(edges, own2, left, right, wide, top, bottom):
    lane = iota(1)
    stop = RIM + 64
    for j in range(8):
        at = pl.ds(8 * j, 8)
        for i in range(3):
            low = roll(left[at, :], -RIM * i, 1)
            high = roll(right[at, :], stop - RIM * i, 1)
            x = jnp.where(lane < RIM * edges[0], low, own2[i, at, :])
            x = jnp.where((lane >= stop) & (lane < stop + RIM * edges[1]), high, x)
            wide[i, at, :] = x
            if 8 * j < RIM:
                top[i, at, :] = x
            if 8 * j >= 64 - RIM:
                bottom[i, pl.ds(8 * j - 64 + RIM, 8), :] = x


def middle_kernel(edges, wide, above, below, *refs):
    kept, message, refs = refs[0:12], refs[12], refs[13:]
    two, three = named_levels((2, 3), kept, refs)
    four = refs[8]
    clear_rows([two[n] for n in "ksbvuweon"], (0, PAD + 112))
    clear_rows([three[n] for n in "ksbvuweon"], (0, PAD + 56))
    lane = iota(1)
    for i, name in enumerate("ksb"):
        for j in range(RIM // 8):
            at = pl.ds(8 * j, 8)
            up = jnp.where(lane < LANES * edges[2], above[i, at, :], 0.0)
            down = jnp.where(lane < LANES * edges[3], below[i, at, :], 0.0)
            two[name][0, pl.ds(PAD + 8 * j, 8), :] = up
            two[name][0, pl.ds(PAD + RIM + 64 + 8 * j, 8), :] = down
        two[name][0, pl.ds(PAD + RIM, 64), :] = wide[i]
    smooth_down(two, 0, 112, 7)
    coarsen_into(two, (three["k"], three["s"], three["b"]), 0, 56)
    smooth_down(three, 0, 56, 7)
    coarsen_into(three, (four.at[0], four.at[1], four.at[2]), 0, 32)
    chooser = pick(lambda r, c: (r == 4 * c) & (c < 28))
    total = choose(jnp.concatenate([four[i, 0, pl.ds(PAD, 32), :] for i in range(3)], axis=0), chooser)
    for i in range(3):
        message[i, :, :] = total[32 * i : 32 * i + 32]


def coarse_join_kernel(edges, message, left, right, wide):
    lane = iota(1)
    for i in range(3):
        for j in range(4):
            at = pl.ds(8 * j, 8)
            low, x, high = roll(left[i, at, :], 2, 1), roll(message[i, at, :], 18, 1), roll(right[i, at, :], 34, 1)
            low = jnp.where((lane >= 2) & (lane < 20 * edges[0]), low, 0.0)
            high = jnp.where(lane < 44 + 18 * edges[1], high, 0.0)
            wide[i, at, :] = jnp.where(lane < 20, low, jnp.where(lane < 44, x, high))


def up_kernel(edges, wide, upper, lower, *refs):
    kept, out, refs = refs[0:24], refs[24], refs[25:]
    four = dict(zip("ksbvudweon", refs[0:10]), step=1)
    five = dict(zip("ksbvudweon", refs[10:20]), step=2)
    levels = [dict(zip(KEPT, kept[6 * depth : 6 * depth + 6])) for depth in range(4)]
    for depth, level in enumerate(levels):
        level.update(zip("uc", refs[20 + 2 * depth : 22 + 2 * depth]), step=STEP[depth])
    from4, coarse_fine = refs[28:30]

    column = lax.broadcasted_iota(jnp.int32, (32, LANES), 1)
    clear_rows([four[n] for n in "ksb"], (PAD, PAD + 56))
    for i, name in enumerate("ksb"):
        four[name][0, pl.ds(PAD + 2, 18), :] = jnp.where(column < LANES * edges[2], upper[i], 0.0)[0:18]
        four[name][0, pl.ds(PAD + 20, 24), :] = wide[i, 2:26, :]
        four[name][0, pl.ds(PAD + 44, 18), :] = jnp.where(column < LANES * edges[3], lower[i], 0.0)[10:28]
    clear_rows([four[n] for n in "kvu"], (0, PAD + 64))
    clear_rows([five[n] for n in "kvu"], (0, PAD + 32))
    smooth_down(four, 0, 64, 4)
    coarsen_into(four, (five["k"], five["s"], five["b"]), 0, 32)
    face_pass(five, PAD, PAD + 32, 4)
    v, u = five["v"], five["u"]
    for _ in range(COARSE_SWEEPS - 1):
        sweep_pass(five, u, v, PAD, PAD + 32, 4)
        v, u = u, v
    correct_pass(u, four["v"], four["v"], PAD, PAD + 32, PAD)
    sweep_pass(four, four["v"], four["u"], PAD, PAD + 64, 4)
    sweep_pass(four, four["u"], four["v"], PAD, PAD + 64, 4)
    from4[0, :, :] = choose(four["v"][0, pl.ds(PAD + 16, 32), :], pick(lambda r, c: r == c // 4 + 18))

    def rise(depth, coarse, first, last, shift, start, stop, height, twice=True):
        level = levels[depth]
        u, c = level["u"], level["c"]
        correct_pass(coarse, level["v"], c, first, last, shift)
        sweep_pass(level, c, u, start, stop, height)
        if twice:
            clear_rows([u], (start - 8, stop))
            sweep_pass(level, u, c, start, stop, height)
        return c

    c = rise(3, from4, 0, 32, -4, 8, 64, 7)
    c = rise(2, c, 8, 64, 8, 24, 104, 5)
    fine = c[0, pl.ds(24, 80), :]
    for t in range(3):
        turn = lambda c: jnp.where(c < 64, 0, 96) if t == 2 else 0
        coarse_fine[t, :, :] = choose(fine, pick(lambda r, c: r == (c + LANES * t) // 4 + RIM - turn(c)))
    c = rise(1, coarse_fine, 0, 80, -8, 16, 160, 6)
    rise(0, c, 16, 160, 8, 24, 312, 12, False)

    level = levels[0]

    def body(row):
        cells = around(level["u"], row, 8, 1)
        for j in range(8):
            for t in range(2):
                value = (1.0 - OMEGA) * cells[t, j][0] + weighted(level, t, rows_at(row, j), cells[t, j])
                out[pl.ds(row + 8 * j - PAD - 32, 8), LANES * t : LANES * (t + 1)] = value

    over_rows(PAD + 32, PAD + 32 + SIZE, 8, body)


def shape_of(*shape):
    return jax.ShapeDtypeStruct(shape, jnp.float32)


def vmem(*shape):
    return pltpu.VMEM(shape, jnp.float32)


HERE = pl.BlockSpec(memory_space=pltpu.VMEM)
SCALARS = pl.BlockSpec(memory_space=pltpu.SMEM)
AWAY = pl.BlockSpec(memory_space=pltpu.HBM)


def cost(flops, count):
    return pl.CostEstimate(flops=flops, bytes_accessed=count, transcendentals=0)


def exchange(up_block, down_block, axis):
    count = lax.axis_size(axis)
    up = [(i, (i + 1) % count) for i in range(count)]
    down = [(j, i) for i, j in up]
    return lax.ppermute(up_block, axis, up), lax.ppermute(down_block, axis, down)


def call(kernel, outs, ins, scratch=(), grant=4, aliases={}):
    return pl.pallas_call(
        kernel,
        out_shape=tuple(shape_of(*shape) for shape in outs),
        in_specs=[SCALARS] + [HERE] * (len(ins) - 1),
        out_specs=(HERE,) * len(outs),
        scratch_shapes=scratch,
        input_output_aliases=aliases,
        cost_estimate=cost(8 * MIB, 4 * MIB),
        compiler_params=pltpu.CompilerParams(vmem_limit_bytes=grant * MIB),
    )(*ins)


def per_device(pressure, source, conductivity, storage):
    blocks = (conductivity, storage, source, pressure)
    x, y = lax.axis_index("gx"), lax.axis_index("gy")
    inside = (y > 0, y < lax.axis_size("gy") - 1, x > 0, x < lax.axis_size("gx") - 1)
    edges = jnp.stack(inside).astype(jnp.int32)
    own, low, high = pl.pallas_call(
        pack_kernel,
        out_shape=(shape_of(4, 2, SIZE, LANES), shape_of(128, LANES), shape_of(128, LANES)),
        in_specs=[AWAY] * 4,
        out_specs=(HERE,) * 3,
        scratch_shapes=[pltpu.SemaphoreType.DMA((8,))],
        cost_estimate=cost(2 * MIB, 2 * MIB),
        compiler_params=pltpu.CompilerParams(vmem_limit_bytes=2 * MIB),
    )(*[pltpu.with_memory_space_constraint(block, pltpu.HBM) for block in blocks])
    before, after = exchange(high, low, "gy")
    shrunk = call(shrink_kernel, [array_of(1)] * 2 + [(2, 64, LANES)] * 2, (edges, own))
    top, bottom = call(edge_kernel, [(4, 3, HALO, LANES)] * 2, (edges, own, before, after, shrunk[3]))
    above, below = exchange(bottom, top, "gx")

    started = call(start_kernel, [array_of(0)] * 10, (edges, own, before, after))
    *kept, own2, low2, high2 = call(
        fine_kernel,
        [array_of(0)] * 10 + [array_of(1)] * 8 + [(3, 64, LANES), (64, LANES), (64, LANES)],
        (edges, above, below, *started, *shrunk),
        [vmem(*array_of(1))] * 2 + [vmem(2, 80 + 2 * PAD, LANES)],
        aliases={3 + n: n for n in range(10)} | {13: 16, 14: 17},
    )
    kept = kept[:6] + kept[10:16]
    left, right = exchange(high2, low2, "gy")
    wide2, top2, bottom2 = call(
        join_kernel, [(3, 64, LANES), (3, RIM, LANES), (3, RIM, LANES)], (edges, own2, left, right)
    )
    above2, below2 = exchange(bottom2, top2, "gx")
    *more, message = call(
        middle_kernel,
        [array_of(2)] * 6 + [array_of(3)] * 6 + [(3, 32, LANES)],
        (edges, wide2, above2, below2),
        [vmem(*array_of(2))] * 4 + [vmem(*array_of(3))] * 4 + [vmem(3, 1, 32 + 2 * PAD, LANES)],
    )

    left, right = exchange(message, message, "gy")
    (wide,) = call(coarse_join_kernel, [(3, 32, LANES)], (edges, message, left, right))
    upper, lower = exchange(wide, wide, "gx")
    return pl.pallas_call(
        up_kernel,
        out_shape=shape_of(SIZE, SIZE),
        in_specs=[SCALARS] + [HERE] * 27,
        out_specs=HERE,
        scratch_shapes=[
            *[vmem(1, 64 + 2 * PAD, LANES)] * 10,
            *[vmem(1, 32 + 2 * PAD, LANES)] * 10,
            *[vmem(*array_of(depth)) for depth in range(4) for _ in range(2)],
            vmem(1, 32, LANES),
            vmem(3, 80, LANES),
        ],
        cost_estimate=cost(40 * MIB, 12 * MIB),
        compiler_params=pltpu.CompilerParams(vmem_limit_bytes=5 * MIB),
    )(edges, wide, upper, lower, *kept, *more)


def solution(mesh):
    placed = (P("gx", "gy"),) * 4
    return jax.shard_map(per_device, mesh=mesh, in_specs=placed, out_specs=P("gx", "gy"), check_vma=False)
```

```python
import jax
import jax.numpy as jnp
from jax import lax
from jax.experimental import pallas as pl
from jax.experimental.pallas import tpu as pltpu
from jax.sharding import PartitionSpec as P

OMEGA = 0.8
COARSE_SWEEPS = 8
SIZE = 256
HALO = 16
RIM = 24
PAD = 8
LANES = 128
MIB = 1 << 20


def iota(axis):
    return lax.broadcasted_iota(jnp.int32, (8, LANES), axis)


def roll(x, amount, axis):
    return pltpu.roll(x, amount % x.shape[axis], axis)


def row_shift(tiles):
    row = iota(0)
    down = [roll(x, 1, 0) for x in tiles[:-1]]
    up = [roll(x, -1, 0) for x in tiles[1:]]
    before = [jnp.where(row == 0, down[j], down[j + 1]) for j in range(len(down) - 1)]
    after = [jnp.where(row == 7, up[j + 1], up[j]) for j in range(len(up) - 1)]
    return before, after


def lane_shift(tiles, step):
    lane = iota(1)
    right = [roll(x, step, 1) for x in tiles]
    left = [roll(x, -step, 1) for x in tiles]
    count = len(tiles)
    before = [jnp.where(lane < step, right[t - 1], right[t]) for t in range(count)]
    after = [jnp.where(lane >= LANES - step, left[(t + 1) % count], left[t]) for t in range(count)]
    return before, after


def around(ref, row, depth, step):
    count = ref.shape[0]
    rows = [[ref[t, pl.ds(row + 8 * j - 8, 8), :] for j in range(depth + 2)] for t in range(count)]
    west, east = zip(*[row_shift(tiles) for tiles in rows])
    cells = {}
    for j in range(depth):
        here = [rows[t][j + 1] for t in range(count)]
        south, north = lane_shift(here, step)
        for t in range(count):
            cells[t, j] = (here[t], west[t][j], east[t][j], south[t], north[t])
    return cells


def over_rows(first, last, depth, body):
    trips = (last - first) // (8 * depth)

    def trip(i, carry):
        body(pl.multiple_of(first + i * 8 * depth, 8))
        return carry

    lax.fori_loop(0, trips, trip, 0)


def rows_at(row, j):
    return pl.ds(row + 8 * j, 8)


def face_pass(level, first, last, depth, guess=None):
    def body(row):
        cells = None if guess is None else around(guess, row, depth, level["step"])
        for (t, j), (k, kw, ke, ks, kn) in around(level["k"], row, depth, level["step"]).items():
            at = rows_at(row, j)
            west, east, south, north = (0.5 * (k + other) for other in (kw, ke, ks, kn))
            stored = level["s"][t, at, :]
            diagonal = (((stored + west) + east) + south) + north
            scale = jnp.where(stored > 0.0, OMEGA / diagonal, 0.0)
            level["d"][t, at, :] = diagonal
            side = scale * level["b"][t, at, :]
            level["b"][t, at, :] = side
            weights = [scale * face for face in (west, east, south, north)]
            for name, weight in zip("weon", weights):
                level[name][t, at, :] = weight
            if cells:
                v, *others = cells[t, j]
                side = side + (1.0 - OMEGA) * v
                for weight, other in zip(weights, others):
                    side = side + weight * other
            level["u"][t, at, :] = side

    over_rows(first, last, depth, body)


def weighted(level, t, at, cell):
    _, vw, ve, vs, vn = cell
    total = level["b"][t, at, :] + level["w"][t, at, :] * vw
    total = total + level["e"][t, at, :] * ve
    total = total + level["o"][t, at, :] * vs
    return total + level["n"][t, at, :] * vn


def sweep_pass(level, source, target, first, last, depth):
    def body(row):
        for (t, j), cell in around(source, row, depth, level["step"]).items():
            at = rows_at(row, j)
            target[t, at, :] = (1.0 - OMEGA) * cell[0] + weighted(level, t, at, cell)

    over_rows(first, last, depth, body)


def residual_pass(level, source, target, first, last, depth):
    def body(row):
        for (t, j), cell in around(source, row, depth, level["step"]).items():
            at = rows_at(row, j)
            gap = (1.0 / OMEGA) * weighted(level, t, at, cell) - cell[0]
            target[t, at, :] = level["d"][t, at, :] * gap

    over_rows(first, last, depth, body)


def pair_sum(source, t, row, step):
    x = source[t, pl.ds(row, 8, stride=2), :] + source[t, pl.ds(row + 1, 8, stride=2), :]
    upper = (iota(1) & step) != 0
    return x + jnp.where(upper, roll(x, step, 1), roll(x, -step, 1))


def coarsen_pass(triples, step, first, last):
    trips = (last - first) // 8
    height = max(n for n in range(1, 9) if trips % n == 0)

    def body(row):
        for j in range(height):
            for source, target, factor in triples:
                for t in range(source.shape[0]):
                    x = pair_sum(source, t, 2 * row + 16 * j + PAD, step)
                    target[t, rows_at(row + PAD, j), :] = x if factor == 1.0 else factor * x

    over_rows(first, last, height, body)


def correct_pass(source, base, target, first, last, shift):
    trips = (last - first) // 8
    height = max(n for n in range(1, 8) if trips % n == 0)

    def body(row):
        for j in range(height):
            for t in range(source.shape[0]):
                x = source[t, rows_at(row, j), :]
                for half in range(2):
                    at = pl.ds(2 * row + 16 * j - shift + half, 8, stride=2)
                    target[t, at, :] = base[t, at, :] + x

    over_rows(first, last, height, body)


def clear_rows(refs, at):
    for ref in refs:
        for row in at:
            for t in range(ref.shape[0]):
                ref[t, pl.ds(row, 8), :] = jnp.zeros((8, LANES), jnp.float32)


TILES = (3, 3, 1, 1)
ROWS = (320, 160, 112, 56)
PLACE = (32, 16, RIM, RIM // 2)
STEP = (1, 2, 1, 2)
KEPT = "vbweon"


def array_of(depth):
    return (TILES[depth], ROWS[depth] + 2 * PAD, LANES)


def pack_kernel(k, s, b, v, own, low, high, sems):
    copies = []
    for i, a in enumerate((k, s, b, v)):
        for t in range(2):
            copies.append(pltpu.make_async_copy(a.at[:, pl.ds(LANES * t, LANES)], own.at[i, t], sems.at[2 * i + t]))
    for copy in copies:
        copy.start()
    for copy in copies:
        copy.wait()

    def body(row):
        lane = iota(1)
        for target, t, shift in ((low, 0, 0), (high, 1, HALO)):
            parts = []
            for half in range(2):
                for i in range(4):
                    x = own[i, t, pl.ds(row + 128 * half, 8), :]
                    amount = shift + 64 * half + HALO * i
                    parts.append(roll(x, amount, 1) if amount else x)
            total = parts[7]
            for n in range(6, -1, -1):
                total = jnp.where(lane < HALO * (n + 1), parts[n], total)
            target[pl.ds(row, 8), :] = total

    over_rows(0, 128, 1, body)


def widened(edges, own, before, after, row, half):
    lane = iota(1)
    left = before[pl.ds(row - 128 * half, 8), :]
    right = after[pl.ds(row - 128 * half, 8), :]
    for i in range(4):
        start = 64 * half + HALO * i
        low, high = roll(left, -HALO - start, 1), roll(right, -start, 1)
        low = jnp.where(lane >= LANES - HALO * edges[0], low, 0.0)
        yield i, 0, own[i, 0, pl.ds(row, 8), :]
        yield i, 1, own[i, 1, pl.ds(row, 8), :]
        yield i, 2, jnp.where(lane < HALO * edges[1], high, low)


def edge_kernel(edges, own, before, after, _, top, bottom):
    for j in range(HALO // 8):
        for target, row, half in ((top, 8 * j, 0), (bottom, SIZE - HALO + 8 * j, 1)):
            for i, t, x in widened(edges, own, before, after, row, half):
                target[i, t, pl.ds(8 * j, 8), :] = x


def pick(rule):
    shape = (LANES, LANES)
    rows = lax.broadcasted_iota(jnp.int32, shape, 0)
    columns = lax.broadcasted_iota(jnp.int32, shape, 1)
    return rule(rows, columns).astype(jnp.float32).astype(jnp.bfloat16)


def choose(x, chooser):
    total = None
    for _ in range(3):
        term = x.astype(jnp.bfloat16)
        part = jnp.dot(term, chooser, preferred_element_type=jnp.float32)
        total = part if total is None else total + part
        x = x - term.astype(jnp.float32)
    return total


def smooth_down(level, first, last, height, guess=None):
    face_pass(level, PAD + first, PAD + last, height, guess)
    sweep_pass(level, level["u"], level["v"], PAD + first, PAD + last, height)
    residual_pass(level, level["v"], level["u"], PAD + first, PAD + last, height)


def coarsen_into(level, goals, first, last):
    triples = tuple(zip((level["k"], level["s"], level["u"]), goals, (0.5, 1.0, 1.0)))
    coarsen_pass(triples, level["step"], first, last)


def named_levels(depths, kept, scratch):
    levels = []
    for n, depth in enumerate(depths):
        level = dict(zip(KEPT, kept[6 * n : 6 * n + 6]), step=STEP[depth])
        level.update(zip("ksud", scratch[4 * n : 4 * n + 4]))
        levels.append(level)
    return levels


def shrink_kernel(edges, own, k1, s1, k2, s2):
    def halve(source, target, step, from_row, to_row, count, factor):
        def body(row):
            for j in range(4):
                for t in range(2):
                    x = pair_sum(source, t, 2 * row + 16 * j + from_row, step)
                    target[t, rows_at(row + to_row, j), :] = factor * x

        over_rows(0, count, 4, body)

    for i, first, second, factor in ((0, k1, k2, 0.5), (1, s1, s2, 1.0)):
        halve(own.at[i], first, 1, 0, PAD + 16, 128, factor)
        halve(first, second, 2, PAD + 16, 0, 64, factor)


ALL = KEPT + "ksud"


def start_kernel(edges, own, before, after, *refs):
    zero = dict(zip(ALL, refs), step=STEP[0])
    frame = [zero[n] for n in "ksbv"]
    for half in range(2):

        def fill(row):
            for j in range(4):
                for i, t, x in widened(edges, own, before, after, row + 8 * j, half):
                    frame[i][t, rows_at(PAD + 32 + row, j), :] = x

        over_rows(128 * half, 128 * half + 128, 4, fill)
    face_pass(zero, PAD + 40, PAD + 280, 5, zero["v"])


def fine_kernel(edges, above, below, *refs):
    k2, s2, refs = refs[12], refs[13], refs[14:]
    zero = dict(zip(ALL, refs[0:10]), step=STEP[0])
    own2, low2, high2, u1, d1, b2 = refs[18:24]
    one = dict(zip(ALL, (*refs[10:18], u1, d1)), step=STEP[1])
    clear_rows([zero[n] for n in "ksbvuweon"], (PAD + 8, PAD + 304))
    clear_rows([one[n] for n in "ksbvuweon"], (PAD, PAD + 152))
    frame = [zero[n] for n in "ksbv"]
    lane = iota(1)
    for i in range(4):
        for t in range(3):
            for j in range(HALO // 8):
                at = pl.ds(8 * j, 8)
                up = jnp.where(lane < LANES * edges[2], above[i, t, at, :], 0.0)
                down = jnp.where(lane < LANES * edges[3], below[i, t, at, :], 0.0)
                frame[i][t, pl.ds(PAD + 32 - HALO + 8 * j, 8), :] = up
                frame[i][t, pl.ds(PAD + 32 + SIZE + 8 * j, 8), :] = down

    face_pass(zero, PAD + 16, PAD + 40, 3, zero["v"])
    face_pass(zero, PAD + 280, PAD + 304, 3, zero["v"])
    sweep_pass(zero, zero["u"], zero["v"], PAD + 16, PAD + 304, 12)
    residual_pass(zero, zero["v"], zero["u"], PAD + 16, PAD + 304, 12)
    pairs = [(zero[n], one[n], factor) for n, factor in (("k", 0.5), ("s", 1.0))]
    third = [(source.at[pl.ds(2, 1)], target.at[pl.ds(2, 1)], factor) for source, target, factor in pairs]
    coarsen_pass([(zero["u"], one["b"], 1.0), *third], 1, 8, 152)
    first = [(source.at[pl.ds(0, 2)], target.at[pl.ds(0, 2)], factor) for source, target, factor in pairs]
    coarsen_pass(first, 1, 8, 16)
    coarsen_pass(first, 1, 144, 152)
    smooth_down(one, 8, 152, 6)
    coarsen_pass([(one["u"].at[pl.ds(0, 2)], b2, 1.0)], 2, 8, 72)

    total = None
    for t in range(2):
        inside = lambda c: (c >= RIM) & (c < RIM + 64)
        chooser = pick(lambda r, c: (r + LANES * t == 4 * (c - RIM)) & inside(c))
        rows = jnp.concatenate([k2[t], s2[t], b2[t, pl.ds(PAD + 8, 64), :]], axis=0)
        part = choose(rows, chooser)
        total = part if total is None else total + part
    for i in range(3):
        own2[i, :, :] = total[64 * i : 64 * i + 64]

    def send(row):
        lane = iota(1)
        for j in range(4):
            at = rows_at(row, j)
            x = [own2[i, at, :] for i in range(3)]
            for target, start in ((low2, RIM), (high2, 64)):
                y = [roll(x[i], RIM * i - start, 1) for i in range(3)]
                target[at, :] = jnp.where(lane < RIM, y[0], jnp.where(lane < 2 * RIM, y[1], y[2]))

    over_rows(0, 64, 4, send)


def join_kernel(edges, own2, left, right, wide, top, bottom):
    lane = iota(1)
    stop = RIM + 64
    for j in range(8):
        at = pl.ds(8 * j, 8)
        for i in range(3):
            low = roll(left[at, :], -RIM * i, 1)
            high = roll(right[at, :], stop - RIM * i, 1)
            x = jnp.where(lane < RIM * edges[0], low, own2[i, at, :])
            x = jnp.where((lane >= stop) & (lane < stop + RIM * edges[1]), high, x)
            wide[i, at, :] = x
            if 8 * j < RIM:
                top[i, at, :] = x
            if 8 * j >= 64 - RIM:
                bottom[i, pl.ds(8 * j - 64 + RIM, 8), :] = x


def middle_kernel(edges, wide, above, below, *refs):
    kept, message, refs = refs[0:12], refs[12], refs[13:]
    two, three = named_levels((2, 3), kept, refs)
    four = refs[8]
    clear_rows([two[n] for n in "ksbvuweon"], (0, PAD + 112))
    clear_rows([three[n] for n in "ksbvuweon"], (0, PAD + 56))
    lane = iota(1)
    for i, name in enumerate("ksb"):
        for j in range(RIM // 8):
            at = pl.ds(8 * j, 8)
            up = jnp.where(lane < LANES * edges[2], above[i, at, :], 0.0)
            down = jnp.where(lane < LANES * edges[3], below[i, at, :], 0.0)
            two[name][0, pl.ds(PAD + 8 * j, 8), :] = up
            two[name][0, pl.ds(PAD + RIM + 64 + 8 * j, 8), :] = down
        two[name][0, pl.ds(PAD + RIM, 64), :] = wide[i]
    smooth_down(two, 0, 112, 14)
    coarsen_into(two, (three["k"], three["s"], three["b"]), 0, 56)
    smooth_down(three, 0, 56, 7)
    coarsen_into(three, (four.at[0], four.at[1], four.at[2]), 0, 32)
    chooser = pick(lambda r, c: (r == 4 * c) & (c < 28))
    total = choose(jnp.concatenate([four[i, 0, pl.ds(PAD, 32), :] for i in range(3)], axis=0), chooser)
    for i in range(3):
        message[i, :, :] = total[32 * i : 32 * i + 32]


def coarse_join_kernel(edges, message, left, right, wide):
    lane = iota(1)
    for i in range(3):
        for j in range(4):
            at = pl.ds(8 * j, 8)
            low, x, high = roll(left[i, at, :], 2, 1), roll(message[i, at, :], 18, 1), roll(right[i, at, :], 34, 1)
            low = jnp.where((lane >= 2) & (lane < 20 * edges[0]), low, 0.0)
            high = jnp.where(lane < 44 + 18 * edges[1], high, 0.0)
            wide[i, at, :] = jnp.where(lane < 20, low, jnp.where(lane < 44, x, high))


def up_kernel(edges, wide, upper, lower, *refs):
    kept, out, refs = refs[0:24], refs[24], refs[25:]
    four = dict(zip("ksbvudweon", refs[0:10]), step=1)
    five = dict(zip("ksbvudweon", refs[10:20]), step=2)
    levels = [dict(zip(KEPT, kept[6 * depth : 6 * depth + 6])) for depth in range(4)]
    for depth, level in enumerate(levels):
        level.update(zip("uc", refs[20 + 2 * depth : 22 + 2 * depth]), step=STEP[depth])
    from4, coarse_fine = refs[28:30]

    column = lax.broadcasted_iota(jnp.int32, (32, LANES), 1)
    clear_rows([four[n] for n in "ksb"], (PAD, PAD + 56))
    for i, name in enumerate("ksb"):
        four[name][0, pl.ds(PAD + 2, 18), :] = jnp.where(column < LANES * edges[2], upper[i], 0.0)[0:18]
        four[name][0, pl.ds(PAD + 20, 24), :] = wide[i, 2:26, :]
        four[name][0, pl.ds(PAD + 44, 18), :] = jnp.where(column < LANES * edges[3], lower[i], 0.0)[10:28]
    clear_rows([four[n] for n in "kvu"], (0, PAD + 64))
    clear_rows([five[n] for n in "kvu"], (0, PAD + 32))
    smooth_down(four, 0, 64, 8)
    coarsen_into(four, (five["k"], five["s"], five["b"]), 0, 32)
    face_pass(five, PAD, PAD + 32, 4)
    v, u = five["v"], five["u"]
    for _ in range(COARSE_SWEEPS - 1):
        sweep_pass(five, u, v, PAD, PAD + 32, 4)
        v, u = u, v
    correct_pass(u, four["v"], four["v"], PAD, PAD + 32, PAD)
    sweep_pass(four, four["v"], four["u"], PAD, PAD + 64, 8)
    sweep_pass(four, four["u"], four["v"], PAD, PAD + 64, 8)
    from4[0, :, :] = choose(four["v"][0, pl.ds(PAD + 16, 32), :], pick(lambda r, c: r == c // 4 + 18))

    def rise(depth, coarse, first, last, shift, start, stop, height, twice=True):
        level = levels[depth]
        u, c = level["u"], level["c"]
        correct_pass(coarse, level["v"], c, first, last, shift)
        sweep_pass(level, c, u, start, stop, height)
        if twice:
            clear_rows([u], (start - 8, stop))
            sweep_pass(level, u, c, start, stop, height)
        return c

    c = rise(3, from4, 0, 32, -4, 8, 64, 7)
    c = rise(2, c, 8, 64, 8, 24, 104, 10)
    fine = c[0, pl.ds(24, 80), :]
    for t in range(3):
        turn = lambda c: jnp.where(c < 64, 0, 96) if t == 2 else 0
        coarse_fine[t, :, :] = choose(fine, pick(lambda r, c: r == (c + LANES * t) // 4 + RIM - turn(c)))
    c = rise(1, coarse_fine, 0, 80, -8, 16, 160, 6)
    rise(0, c, 16, 160, 8, 24, 312, 12, False)

    level = levels[0]

    def body(row):
        cells = around(level["u"], row, 8, 1)
        for j in range(8):
            for t in range(2):
                value = (1.0 - OMEGA) * cells[t, j][0] + weighted(level, t, rows_at(row, j), cells[t, j])
                out[pl.ds(row + 8 * j - PAD - 32, 8), LANES * t : LANES * (t + 1)] = value

    over_rows(PAD + 32, PAD + 32 + SIZE, 8, body)


def shape_of(*shape):
    return jax.ShapeDtypeStruct(shape, jnp.float32)


def vmem(*shape):
    return pltpu.VMEM(shape, jnp.float32)


HERE = pl.BlockSpec(memory_space=pltpu.VMEM)
SCALARS = pl.BlockSpec(memory_space=pltpu.SMEM)
AWAY = pl.BlockSpec(memory_space=pltpu.HBM)


def cost(flops, count):
    return pl.CostEstimate(flops=flops, bytes_accessed=count, transcendentals=0)


def exchange(up_block, down_block, axis):
    count = lax.axis_size(axis)
    up = [(i, (i + 1) % count) for i in range(count)]
    down = [(j, i) for i, j in up]
    return lax.ppermute(up_block, axis, up), lax.ppermute(down_block, axis, down)


def call(kernel, outs, ins, scratch=(), grant=4, aliases={}):
    return pl.pallas_call(
        kernel,
        out_shape=tuple(shape_of(*shape) for shape in outs),
        in_specs=[SCALARS] + [HERE] * (len(ins) - 1),
        out_specs=(HERE,) * len(outs),
        scratch_shapes=scratch,
        input_output_aliases=aliases,
        cost_estimate=cost(8 * MIB, 4 * MIB),
        compiler_params=pltpu.CompilerParams(vmem_limit_bytes=grant * MIB),
    )(*ins)


def per_device(pressure, source, conductivity, storage):
    blocks = (conductivity, storage, source, pressure)
    x, y = lax.axis_index("gx"), lax.axis_index("gy")
    inside = (y > 0, y < lax.axis_size("gy") - 1, x > 0, x < lax.axis_size("gx") - 1)
    edges = jnp.stack(inside).astype(jnp.int32)
    own, low, high = pl.pallas_call(
        pack_kernel,
        out_shape=(shape_of(4, 2, SIZE, LANES), shape_of(128, LANES), shape_of(128, LANES)),
        in_specs=[AWAY] * 4,
        out_specs=(HERE,) * 3,
        scratch_shapes=[pltpu.SemaphoreType.DMA((8,))],
        cost_estimate=cost(2 * MIB, 2 * MIB),
        compiler_params=pltpu.CompilerParams(vmem_limit_bytes=2 * MIB),
    )(*[pltpu.with_memory_space_constraint(block, pltpu.HBM) for block in blocks])
    before, after = exchange(high, low, "gy")
    shrunk = call(shrink_kernel, [array_of(1)] * 2 + [(2, 64, LANES)] * 2, (edges, own))
    top, bottom = call(edge_kernel, [(4, 3, HALO, LANES)] * 2, (edges, own, before, after, shrunk[3]))
    above, below = exchange(bottom, top, "gx")

    started = call(start_kernel, [array_of(0)] * 10, (edges, own, before, after))
    *kept, own2, low2, high2 = call(
        fine_kernel,
        [array_of(0)] * 10 + [array_of(1)] * 8 + [(3, 64, LANES), (64, LANES), (64, LANES)],
        (edges, above, below, *started, *shrunk),
        [vmem(*array_of(1))] * 2 + [vmem(2, 80 + 2 * PAD, LANES)],
        aliases={3 + n: n for n in range(10)} | {13: 16, 14: 17},
    )
    kept = kept[:6] + kept[10:16]
    left, right = exchange(high2, low2, "gy")
    wide2, top2, bottom2 = call(
        join_kernel, [(3, 64, LANES), (3, RIM, LANES), (3, RIM, LANES)], (edges, own2, left, right)
    )
    above2, below2 = exchange(bottom2, top2, "gx")
    *more, message = call(
        middle_kernel,
        [array_of(2)] * 6 + [array_of(3)] * 6 + [(3, 32, LANES)],
        (edges, wide2, above2, below2),
        [vmem(*array_of(2))] * 4 + [vmem(*array_of(3))] * 4 + [vmem(3, 1, 32 + 2 * PAD, LANES)],
    )

    left, right = exchange(message, message, "gy")
    (wide,) = call(coarse_join_kernel, [(3, 32, LANES)], (edges, message, left, right))
    upper, lower = exchange(wide, wide, "gx")
    return pl.pallas_call(
        up_kernel,
        out_shape=shape_of(SIZE, SIZE),
        in_specs=[SCALARS] + [HERE] * 27,
        out_specs=HERE,
        scratch_shapes=[
            *[vmem(1, 64 + 2 * PAD, LANES)] * 10,
            *[vmem(1, 32 + 2 * PAD, LANES)] * 10,
            *[vmem(*array_of(depth)) for depth in range(4) for _ in range(2)],
            vmem(1, 32, LANES),
            vmem(3, 80, LANES),
        ],
        cost_estimate=cost(40 * MIB, 12 * MIB),
        compiler_params=pltpu.CompilerParams(vmem_limit_bytes=5 * MIB),
    )(edges, wide, upper, lower, *kept, *more)


def solution(mesh):
    placed = (P("gx", "gy"),) * 4
    return jax.shard_map(per_device, mesh=mesh, in_specs=placed, out_specs=P("gx", "gy"), check_vma=False)
```

```python
import jax
import jax.numpy as jnp
from jax import lax
from jax.experimental import pallas as pl
from jax.experimental.pallas import tpu as pltpu
from jax.sharding import PartitionSpec as P

OMEGA = 0.8
COARSE_SWEEPS = 8
SIZE = 256
HALO = 16
RIM = 24
PAD = 8
LANES = 128
MIB = 1 << 20


def iota(axis):
    return lax.broadcasted_iota(jnp.int32, (8, LANES), axis)


def roll(x, amount, axis):
    return pltpu.roll(x, amount % x.shape[axis], axis)


def row_shift(tiles):
    row = iota(0)
    down = [roll(x, 1, 0) for x in tiles[:-1]]
    up = [roll(x, -1, 0) for x in tiles[1:]]
    before = [jnp.where(row == 0, down[j], down[j + 1]) for j in range(len(down) - 1)]
    after = [jnp.where(row == 7, up[j + 1], up[j]) for j in range(len(up) - 1)]
    return before, after


def lane_shift(tiles, step):
    lane = iota(1)
    right = [roll(x, step, 1) for x in tiles]
    left = [roll(x, -step, 1) for x in tiles]
    count = len(tiles)
    before = [jnp.where(lane < step, right[t - 1], right[t]) for t in range(count)]
    after = [jnp.where(lane >= LANES - step, left[(t + 1) % count], left[t]) for t in range(count)]
    return before, after


def around(ref, row, depth, step):
    count = ref.shape[0]
    rows = [[ref[t, pl.ds(row + 8 * j - 8, 8), :] for j in range(depth + 2)] for t in range(count)]
    west, east = zip(*[row_shift(tiles) for tiles in rows])
    cells = {}
    for j in range(depth):
        here = [rows[t][j + 1] for t in range(count)]
        south, north = lane_shift(here, step)
        for t in range(count):
            cells[t, j] = (here[t], west[t][j], east[t][j], south[t], north[t])
    return cells


def over_rows(first, last, depth, body):
    trips = (last - first) // (8 * depth)

    def trip(i, carry):
        body(pl.multiple_of(first + i * 8 * depth, 8))
        return carry

    lax.fori_loop(0, trips, trip, 0)


def rows_at(row, j):
    return pl.ds(row + 8 * j, 8)


def face_pass(level, first, last, depth, guess=None):
    def body(row):
        cells = None if guess is None else around(guess, row, depth, level["step"])
        for (t, j), (k, kw, ke, ks, kn) in around(level["k"], row, depth, level["step"]).items():
            at = rows_at(row, j)
            west, east, south, north = (0.5 * (k + other) for other in (kw, ke, ks, kn))
            stored = level["s"][t, at, :]
            diagonal = (((stored + west) + east) + south) + north
            scale = jnp.where(stored > 0.0, OMEGA / diagonal, 0.0)
            level["d"][t, at, :] = diagonal
            side = scale * level["b"][t, at, :]
            level["b"][t, at, :] = side
            weights = [scale * face for face in (west, east, south, north)]
            for name, weight in zip("weon", weights):
                level[name][t, at, :] = weight
            if cells:
                v, *others = cells[t, j]
                side = side + (1.0 - OMEGA) * v
                for weight, other in zip(weights, others):
                    side = side + weight * other
            level["u"][t, at, :] = side

    over_rows(first, last, depth, body)


def weighted(level, t, at, cell):
    _, vw, ve, vs, vn = cell
    total = level["b"][t, at, :] + level["w"][t, at, :] * vw
    total = total + level["e"][t, at, :] * ve
    total = total + level["o"][t, at, :] * vs
    return total + level["n"][t, at, :] * vn


def sweep_pass(level, source, target, first, last, depth):
    def body(row):
        for (t, j), cell in around(source, row, depth, level["step"]).items():
            at = rows_at(row, j)
            target[t, at, :] = (1.0 - OMEGA) * cell[0] + weighted(level, t, at, cell)

    over_rows(first, last, depth, body)


def residual_pass(level, source, target, first, last, depth):
    def body(row):
        for (t, j), cell in around(source, row, depth, level["step"]).items():
            at = rows_at(row, j)
            gap = (1.0 / OMEGA) * weighted(level, t, at, cell) - cell[0]
            target[t, at, :] = level["d"][t, at, :] * gap

    over_rows(first, last, depth, body)


def pair_sum(source, t, row, step):
    x = source[t, pl.ds(row, 8, stride=2), :] + source[t, pl.ds(row + 1, 8, stride=2), :]
    upper = (iota(1) & step) != 0
    return x + jnp.where(upper, roll(x, step, 1), roll(x, -step, 1))


def coarsen_pass(triples, step, first, last):
    trips = (last - first) // 8
    height = max(n for n in range(1, 9) if trips % n == 0)

    def body(row):
        for j in range(height):
            for source, target, factor in triples:
                for t in range(source.shape[0]):
                    x = pair_sum(source, t, 2 * row + 16 * j + PAD, step)
                    target[t, rows_at(row + PAD, j), :] = x if factor == 1.0 else factor * x

    over_rows(first, last, height, body)


def correct_pass(source, base, target, first, last, shift):
    trips = (last - first) // 8
    height = max(n for n in range(1, 8) if trips % n == 0)

    def body(row):
        for j in range(height):
            for t in range(source.shape[0]):
                x = source[t, rows_at(row, j), :]
                for half in range(2):
                    at = pl.ds(2 * row + 16 * j - shift + half, 8, stride=2)
                    target[t, at, :] = base[t, at, :] + x

    over_rows(first, last, height, body)


def clear_rows(refs, at):
    for ref in refs:
        for row in at:
            for t in range(ref.shape[0]):
                ref[t, pl.ds(row, 8), :] = jnp.zeros((8, LANES), jnp.float32)


TILES = (3, 3, 1, 1)
ROWS = (320, 160, 112, 56)
PLACE = (32, 16, RIM, RIM // 2)
STEP = (1, 2, 1, 2)
KEPT = "vbweon"


def array_of(depth):
    return (TILES[depth], ROWS[depth] + 2 * PAD, LANES)


def pack_kernel(k, s, b, v, own, low, high, sems):
    copies = []
    for i, a in enumerate((k, s, b, v)):
        for t in range(2):
            copies.append(pltpu.make_async_copy(a.at[:, pl.ds(LANES * t, LANES)], own.at[i, t], sems.at[2 * i + t]))
    for copy in copies:
        copy.start()
    for copy in copies:
        copy.wait()

    def body(row):
        lane = iota(1)
        for target, t, shift in ((low, 0, 0), (high, 1, HALO)):
            parts = []
            for half in range(2):
                for i in range(4):
                    x = own[i, t, pl.ds(row + 128 * half, 8), :]
                    amount = shift + 64 * half + HALO * i
                    parts.append(roll(x, amount, 1) if amount else x)
            total = parts[7]
            for n in range(6, -1, -1):
                total = jnp.where(lane < HALO * (n + 1), parts[n], total)
            target[pl.ds(row, 8), :] = total

    over_rows(0, 128, 1, body)


def widened(edges, own, before, after, row, half):
    lane = iota(1)
    left = before[pl.ds(row - 128 * half, 8), :]
    right = after[pl.ds(row - 128 * half, 8), :]
    for i in range(4):
        start = 64 * half + HALO * i
        low, high = roll(left, -HALO - start, 1), roll(right, -start, 1)
        low = jnp.where(lane >= LANES - HALO * edges[0], low, 0.0)
        yield i, 0, own[i, 0, pl.ds(row, 8), :]
        yield i, 1, own[i, 1, pl.ds(row, 8), :]
        yield i, 2, jnp.where(lane < HALO * edges[1], high, low)


def edge_kernel(edges, own, before, after, _, top, bottom):
    for j in range(HALO // 8):
        for target, row, half in ((top, 8 * j, 0), (bottom, SIZE - HALO + 8 * j, 1)):
            for i, t, x in widened(edges, own, before, after, row, half):
                target[i, t, pl.ds(8 * j, 8), :] = x


def pick(rule):
    shape = (LANES, LANES)
    rows = lax.broadcasted_iota(jnp.int32, shape, 0)
    columns = lax.broadcasted_iota(jnp.int32, shape, 1)
    return rule(rows, columns).astype(jnp.float32).astype(jnp.bfloat16)


def choose(x, chooser):
    total = None
    for _ in range(3):
        term = x.astype(jnp.bfloat16)
        part = jnp.dot(term, chooser, preferred_element_type=jnp.float32)
        total = part if total is None else total + part
        x = x - term.astype(jnp.float32)
    return total


def smooth_down(level, first, last, height, guess=None):
    face_pass(level, PAD + first, PAD + last, height, guess)
    sweep_pass(level, level["u"], level["v"], PAD + first, PAD + last, height)
    residual_pass(level, level["v"], level["u"], PAD + first, PAD + last, height)


def coarsen_into(level, goals, first, last):
    triples = tuple(zip((level["k"], level["s"], level["u"]), goals, (0.5, 1.0, 1.0)))
    coarsen_pass(triples, level["step"], first, last)


def named_levels(depths, kept, scratch):
    levels = []
    for n, depth in enumerate(depths):
        level = dict(zip(KEPT, kept[6 * n : 6 * n + 6]), step=STEP[depth])
        level.update(zip("ksud", scratch[4 * n : 4 * n + 4]))
        levels.append(level)
    return levels


def shrink_kernel(edges, own, k1, s1, k2, s2):
    def halve(source, target, step, from_row, to_row, count, factor):
        def body(row):
            for j in range(4):
                for t in range(2):
                    x = pair_sum(source, t, 2 * row + 16 * j + from_row, step)
                    target[t, rows_at(row + to_row, j), :] = factor * x

        over_rows(0, count, 4, body)

    for i, first, second, factor in ((0, k1, k2, 0.5), (1, s1, s2, 1.0)):
        halve(own.at[i], first, 1, 0, PAD + 16, 128, factor)
        halve(first, second, 2, PAD + 16, 0, 64, factor)


ALL = KEPT + "ksud"


def start_kernel(edges, own, before, after, *refs):
    zero = dict(zip(ALL, refs), step=STEP[0])
    frame = [zero[n] for n in "ksbv"]
    for half in range(2):

        def fill(row):
            for j in range(4):
                for i, t, x in widened(edges, own, before, after, row + 8 * j, half):
                    frame[i][t, rows_at(PAD + 32 + row, j), :] = x

        over_rows(128 * half, 128 * half + 128, 4, fill)
    face_pass(zero, PAD + 40, PAD + 280, 5, zero["v"])


def fine_kernel(edges, above, below, *refs):
    k2, s2, refs = refs[12], refs[13], refs[14:]
    zero = dict(zip(ALL, refs[0:10]), step=STEP[0])
    own2, low2, high2, u1, d1, b2 = refs[18:24]
    one = dict(zip(ALL, (*refs[10:18], u1, d1)), step=STEP[1])
    clear_rows([zero[n] for n in "ksbvuweon"], (PAD + 8, PAD + 304))
    clear_rows([one[n] for n in "ksbvuweon"], (PAD, PAD + 152))
    frame = [zero[n] for n in "ksbv"]
    lane = iota(1)
    for i in range(4):
        for t in range(3):
            for j in range(HALO // 8):
                at = pl.ds(8 * j, 8)
                up = jnp.where(lane < LANES * edges[2], above[i, t, at, :], 0.0)
                down = jnp.where(lane < LANES * edges[3], below[i, t, at, :], 0.0)
                frame[i][t, pl.ds(PAD + 32 - HALO + 8 * j, 8), :] = up
                frame[i][t, pl.ds(PAD + 32 + SIZE + 8 * j, 8), :] = down

    face_pass(zero, PAD + 16, PAD + 40, 3, zero["v"])
    face_pass(zero, PAD + 280, PAD + 304, 3, zero["v"])
    sweep_pass(zero, zero["u"], zero["v"], PAD + 16, PAD + 304, 12)
    residual_pass(zero, zero["v"], zero["u"], PAD + 16, PAD + 304, 12)
    pairs = [(zero[n], one[n], factor) for n, factor in (("k", 0.5), ("s", 1.0))]
    third = [(source.at[pl.ds(2, 1)], target.at[pl.ds(2, 1)], factor) for source, target, factor in pairs]
    coarsen_pass([(zero["u"], one["b"], 1.0), *third], 1, 8, 152)
    first = [(source.at[pl.ds(0, 2)], target.at[pl.ds(0, 2)], factor) for source, target, factor in pairs]
    coarsen_pass(first, 1, 8, 16)
    coarsen_pass(first, 1, 144, 152)
    smooth_down(one, 8, 152, 18)
    coarsen_pass([(one["u"].at[pl.ds(0, 2)], b2, 1.0)], 2, 8, 72)

    total = None
    for t in range(2):
        inside = lambda c: (c >= RIM) & (c < RIM + 64)
        chooser = pick(lambda r, c: (r + LANES * t == 4 * (c - RIM)) & inside(c))
        rows = jnp.concatenate([k2[t], s2[t], b2[t, pl.ds(PAD + 8, 64), :]], axis=0)
        part = choose(rows, chooser)
        total = part if total is None else total + part
    for i in range(3):
        own2[i, :, :] = total[64 * i : 64 * i + 64]

    def send(row):
        lane = iota(1)
        for j in range(4):
            at = rows_at(row, j)
            x = [own2[i, at, :] for i in range(3)]
            for target, start in ((low2, RIM), (high2, 64)):
                y = [roll(x[i], RIM * i - start, 1) for i in range(3)]
                target[at, :] = jnp.where(lane < RIM, y[0], jnp.where(lane < 2 * RIM, y[1], y[2]))

    over_rows(0, 64, 4, send)


def join_kernel(edges, own2, left, right, wide, top, bottom):
    lane = iota(1)
    stop = RIM + 64
    for j in range(8):
        at = pl.ds(8 * j, 8)
        for i in range(3):
            low = roll(left[at, :], -RIM * i, 1)
            high = roll(right[at, :], stop - RIM * i, 1)
            x = jnp.where(lane < RIM * edges[0], low, own2[i, at, :])
            x = jnp.where((lane >= stop) & (lane < stop + RIM * edges[1]), high, x)
            wide[i, at, :] = x
            if 8 * j < RIM:
                top[i, at, :] = x
            if 8 * j >= 64 - RIM:
                bottom[i, pl.ds(8 * j - 64 + RIM, 8), :] = x


def middle_kernel(edges, wide, above, below, *refs):
    kept, message, refs = refs[0:12], refs[12], refs[13:]
    two, three = named_levels((2, 3), kept, refs)
    four = refs[8]
    clear_rows([two[n] for n in "ksbvuweon"], (0, PAD + 112))
    clear_rows([three[n] for n in "ksbvuweon"], (0, PAD + 56))
    lane = iota(1)
    for i, name in enumerate("ksb"):
        for j in range(RIM // 8):
            at = pl.ds(8 * j, 8)
            up = jnp.where(lane < LANES * edges[2], above[i, at, :], 0.0)
            down = jnp.where(lane < LANES * edges[3], below[i, at, :], 0.0)
            two[name][0, pl.ds(PAD + 8 * j, 8), :] = up
            two[name][0, pl.ds(PAD + RIM + 64 + 8 * j, 8), :] = down
        two[name][0, pl.ds(PAD + RIM, 64), :] = wide[i]
    smooth_down(two, 0, 112, 14)
    coarsen_into(two, (three["k"], three["s"], three["b"]), 0, 56)
    smooth_down(three, 0, 56, 7)
    coarsen_into(three, (four.at[0], four.at[1], four.at[2]), 0, 32)
    chooser = pick(lambda r, c: (r == 4 * c) & (c < 28))
    total = choose(jnp.concatenate([four[i, 0, pl.ds(PAD, 32), :] for i in range(3)], axis=0), chooser)
    for i in range(3):
        message[i, :, :] = total[32 * i : 32 * i + 32]


def coarse_join_kernel(edges, message, left, right, wide):
    lane = iota(1)
    for i in range(3):
        for j in range(4):
            at = pl.ds(8 * j, 8)
            low, x, high = roll(left[i, at, :], 2, 1), roll(message[i, at, :], 18, 1), roll(right[i, at, :], 34, 1)
            low = jnp.where((lane >= 2) & (lane < 20 * edges[0]), low, 0.0)
            high = jnp.where(lane < 44 + 18 * edges[1], high, 0.0)
            wide[i, at, :] = jnp.where(lane < 20, low, jnp.where(lane < 44, x, high))


def up_kernel(edges, wide, upper, lower, *refs):
    kept, out, refs = refs[0:24], refs[24], refs[25:]
    four = dict(zip("ksbvudweon", refs[0:10]), step=1)
    five = dict(zip("ksbvudweon", refs[10:20]), step=2)
    levels = [dict(zip(KEPT, kept[6 * depth : 6 * depth + 6])) for depth in range(4)]
    for depth, level in enumerate(levels):
        level.update(zip("uc", refs[20 + 2 * depth : 22 + 2 * depth]), step=STEP[depth])
    from4, coarse_fine = refs[28:30]

    column = lax.broadcasted_iota(jnp.int32, (32, LANES), 1)
    clear_rows([four[n] for n in "ksb"], (PAD, PAD + 56))
    for i, name in enumerate("ksb"):
        four[name][0, pl.ds(PAD + 2, 18), :] = jnp.where(column < LANES * edges[2], upper[i], 0.0)[0:18]
        four[name][0, pl.ds(PAD + 20, 24), :] = wide[i, 2:26, :]
        four[name][0, pl.ds(PAD + 44, 18), :] = jnp.where(column < LANES * edges[3], lower[i], 0.0)[10:28]
    clear_rows([four[n] for n in "kvu"], (0, PAD + 64))
    clear_rows([five[n] for n in "kvu"], (0, PAD + 32))
    smooth_down(four, 0, 64, 8)
    coarsen_into(four, (five["k"], five["s"], five["b"]), 0, 32)
    face_pass(five, PAD, PAD + 32, 4)
    v, u = five["v"], five["u"]
    for _ in range(COARSE_SWEEPS - 1):
        sweep_pass(five, u, v, PAD, PAD + 32, 4)
        v, u = u, v
    correct_pass(u, four["v"], four["v"], PAD, PAD + 32, PAD)
    sweep_pass(four, four["v"], four["u"], PAD, PAD + 64, 8)
    sweep_pass(four, four["u"], four["v"], PAD, PAD + 64, 8)
    from4[0, :, :] = choose(four["v"][0, pl.ds(PAD + 16, 32), :], pick(lambda r, c: r == c // 4 + 18))

    def rise(depth, coarse, first, last, shift, start, stop, height, twice=True):
        level = levels[depth]
        u, c = level["u"], level["c"]
        correct_pass(coarse, level["v"], c, first, last, shift)
        sweep_pass(level, c, u, start, stop, height)
        if twice:
            clear_rows([u], (start - 8, stop))
            sweep_pass(level, u, c, start, stop, height)
        return c

    c = rise(3, from4, 0, 32, -4, 8, 64, 7)
    c = rise(2, c, 8, 64, 8, 24, 104, 10)
    fine = c[0, pl.ds(24, 80), :]
    for t in range(3):
        turn = lambda c: jnp.where(c < 64, 0, 96) if t == 2 else 0
        coarse_fine[t, :, :] = choose(fine, pick(lambda r, c: r == (c + LANES * t) // 4 + RIM - turn(c)))
    c = rise(1, coarse_fine, 0, 80, -8, 16, 160, 18)
    rise(0, c, 16, 160, 8, 24, 312, 12, False)

    level = levels[0]

    def body(row):
        cells = around(level["u"], row, 8, 1)
        for j in range(8):
            for t in range(2):
                value = (1.0 - OMEGA) * cells[t, j][0] + weighted(level, t, rows_at(row, j), cells[t, j])
                out[pl.ds(row + 8 * j - PAD - 32, 8), LANES * t : LANES * (t + 1)] = value

    over_rows(PAD + 32, PAD + 32 + SIZE, 8, body)


def shape_of(*shape):
    return jax.ShapeDtypeStruct(shape, jnp.float32)


def vmem(*shape):
    return pltpu.VMEM(shape, jnp.float32)


HERE = pl.BlockSpec(memory_space=pltpu.VMEM)
SCALARS = pl.BlockSpec(memory_space=pltpu.SMEM)
AWAY = pl.BlockSpec(memory_space=pltpu.HBM)


def cost(flops, count):
    return pl.CostEstimate(flops=flops, bytes_accessed=count, transcendentals=0)


def exchange(up_block, down_block, axis):
    count = lax.axis_size(axis)
    up = [(i, (i + 1) % count) for i in range(count)]
    down = [(j, i) for i, j in up]
    return lax.ppermute(up_block, axis, up), lax.ppermute(down_block, axis, down)


def call(kernel, outs, ins, scratch=(), grant=4, aliases={}):
    return pl.pallas_call(
        kernel,
        out_shape=tuple(shape_of(*shape) for shape in outs),
        in_specs=[SCALARS] + [HERE] * (len(ins) - 1),
        out_specs=(HERE,) * len(outs),
        scratch_shapes=scratch,
        input_output_aliases=aliases,
        cost_estimate=cost(8 * MIB, 4 * MIB),
        compiler_params=pltpu.CompilerParams(vmem_limit_bytes=grant * MIB),
    )(*ins)


def per_device(pressure, source, conductivity, storage):
    blocks = (conductivity, storage, source, pressure)
    x, y = lax.axis_index("gx"), lax.axis_index("gy")
    inside = (y > 0, y < lax.axis_size("gy") - 1, x > 0, x < lax.axis_size("gx") - 1)
    edges = jnp.stack(inside).astype(jnp.int32)
    own, low, high = pl.pallas_call(
        pack_kernel,
        out_shape=(shape_of(4, 2, SIZE, LANES), shape_of(128, LANES), shape_of(128, LANES)),
        in_specs=[AWAY] * 4,
        out_specs=(HERE,) * 3,
        scratch_shapes=[pltpu.SemaphoreType.DMA((8,))],
        cost_estimate=cost(2 * MIB, 2 * MIB),
        compiler_params=pltpu.CompilerParams(vmem_limit_bytes=2 * MIB),
    )(*[pltpu.with_memory_space_constraint(block, pltpu.HBM) for block in blocks])
    before, after = exchange(high, low, "gy")
    shrunk = call(shrink_kernel, [array_of(1)] * 2 + [(2, 64, LANES)] * 2, (edges, own))
    top, bottom = call(edge_kernel, [(4, 3, HALO, LANES)] * 2, (edges, own, before, after, shrunk[3]))
    above, below = exchange(bottom, top, "gx")

    started = call(start_kernel, [array_of(0)] * 10, (edges, own, before, after))
    *kept, own2, low2, high2 = call(
        fine_kernel,
        [array_of(0)] * 10 + [array_of(1)] * 8 + [(3, 64, LANES), (64, LANES), (64, LANES)],
        (edges, above, below, *started, *shrunk),
        [vmem(*array_of(1))] * 2 + [vmem(2, 80 + 2 * PAD, LANES)],
        aliases={3 + n: n for n in range(10)} | {13: 16, 14: 17},
    )
    kept = kept[:6] + kept[10:16]
    left, right = exchange(high2, low2, "gy")
    wide2, top2, bottom2 = call(
        join_kernel, [(3, 64, LANES), (3, RIM, LANES), (3, RIM, LANES)], (edges, own2, left, right)
    )
    above2, below2 = exchange(bottom2, top2, "gx")
    *more, message = call(
        middle_kernel,
        [array_of(2)] * 6 + [array_of(3)] * 6 + [(3, 32, LANES)],
        (edges, wide2, above2, below2),
        [vmem(*array_of(2))] * 4 + [vmem(*array_of(3))] * 4 + [vmem(3, 1, 32 + 2 * PAD, LANES)],
    )

    left, right = exchange(message, message, "gy")
    (wide,) = call(coarse_join_kernel, [(3, 32, LANES)], (edges, message, left, right))
    upper, lower = exchange(wide, wide, "gx")
    return pl.pallas_call(
        up_kernel,
        out_shape=shape_of(SIZE, SIZE),
        in_specs=[SCALARS] + [HERE] * 27,
        out_specs=HERE,
        scratch_shapes=[
            *[vmem(1, 64 + 2 * PAD, LANES)] * 10,
            *[vmem(1, 32 + 2 * PAD, LANES)] * 10,
            *[vmem(*array_of(depth)) for depth in range(4) for _ in range(2)],
            vmem(1, 32, LANES),
            vmem(3, 80, LANES),
        ],
        cost_estimate=cost(40 * MIB, 12 * MIB),
        compiler_params=pltpu.CompilerParams(vmem_limit_bytes=5 * MIB),
    )(edges, wide, upper, lower, *kept, *more)


def solution(mesh):
    placed = (P("gx", "gy"),) * 4
    return jax.shard_map(per_device, mesh=mesh, in_specs=placed, out_specs=P("gx", "gy"), check_vma=False)
```
